128 devices in a mesh: seq: 16 (over y, x), exp: 8 (over z, core).
Axes of the slice: x: 4, y: 4, z: 4, core: 2. Of those that a mesh axis runs over, the one named last changes fastest.
Arguments:
- queries: bfloat16 [2048, 8192], P('seq', 'exp'), may hold values from -0.5 to 0.5
- keys: bfloat16 [2048, 8192], P('seq', 'exp'), may hold values from -0.5 to 0.5
- values: bfloat16 [2048, 8192], P('seq', 'exp'), may hold values from -6 to 6
- attn_grad: bfloat16 [2048, 8192], P('seq', 'exp'), may hold values from -6 to 6
- log_decay: float32 [2048, 64], P('seq', 'exp'), may hold values from -0.75 to 0, as said below
- moe_grad: bfloat16 [2048, 6144], P('seq', 'exp'), may hold values from -6 to 6
- gate_probs: bfloat16 [2048, 2], P('seq'), may hold values from 0.099609375 to 0.8984375
- expert_ids: int32 [2048, 2], P('seq'), may hold values from 0 to 7, all different within a row; in each aligned block of 128 rows (0 to 127, 128 to 255, ...) at most 48 rows name the same one
- hidden_acts: bfloat16 [8, 768, 9216], P('exp', None, 'seq'), may hold values from -0.3125 to 0.3125
- down_weight: bfloat16 [8, 9216, 6144], P('exp', 'seq'), may hold values from -0.0625 to 0.0625
Outputs:
- query_grad: bfloat16 [2048, 8192], P('seq', 'exp')
- key_grad: bfloat16 [2048, 8192], P('seq', 'exp')
- value_grad: bfloat16 [2048, 8192], P('seq', 'exp')
- hidden_grad: bfloat16 [8, 768, 9216], P('exp', None, 'seq')
- weight_grad: bfloat16 [8, 9216, 6144], P('exp', 'seq')
- gate_grad: float32 [2048, 2], P('seq')
The draws below stay inside these ranges and needn't reach their ends.
Inputs may be any that keep to these rules, and one draw needn't show every extreme that they name: `expert_ids`: each row names 2 different experts. In the 128 rows of one index of seq no expert is named by more than 48 rows, and every draw has such a block where some expert is named by exactly 48 rows. `log_decay`: log decay of each head at each position; never positive.
All inputs are finite; a program needn't handle non-finite values.
Results may differ from the reference program's by a relative error of at most 0.005.
Values may be sent and summed in bfloat16 or wider, within the bound.
A program may use at most 128 MiB of HBM per device.

```python
import math
import jax
import jax.numpy as jnp
import numpy as np
from jax import lax

D = 6144
FF = 9216
HEAD_COUNT = 64
HEAD_DIM = 128
TOP = 2
TOK_DEV = 128
EXPERTS = 8
TOKEN_COUNT = 2048
CAP = 48
SLOTS = 768
N_SEQ = 16


def draw_log_decay(key, part):
    key_sluggish, key_multiplier, key_spike, key_discard = jax.random.split(jax.random.fold_in(key, 7), 4)
    slow_share = 0.5
    factor = jnp.exp(jax.random.uniform(key_multiplier, (TOKEN_COUNT, HEAD_COUNT), jnp.float32, -0.6931, 0.6931))
    slow_heads = jax.random.uniform(key_sluggish, (HEAD_COUNT,), jnp.float32) < slow_share
    base_rate = jnp.where(slow_heads, 0.6 / TOKEN_COUNT, 1.0 / 40.0)
    decay_speed = -base_rate[None, :] * factor
    spike_location = jax.random.randint(key_spike, (3,), 0, TOKEN_COUNT)
    token_position = jnp.arange(TOKEN_COUNT)
    spike_occurs = jnp.any(token_position[:, None] == spike_location[None, :], axis=1)
    spike_discard = jnp.log(jax.random.uniform(key_discard, (TOKEN_COUNT, HEAD_COUNT), jnp.float32, 0.5, 0.8))
    return jnp.where(spike_occurs[:, None], decay_speed + spike_discard, decay_speed).astype(jnp.float32)


def steps_of(stream_key, extent, shards, smallest, largest):
    factor_of = 1.0
    for axis_at, parts in shards:
        draws = jax.random.uniform(jax.random.fold_in(jax.random.fold_in(stream_key, 6), axis_at), (parts,), jnp.float32, smallest / len(shards), largest / len(shards))
        factor_of = factor_of * jnp.repeat(jnp.exp(draws), extent[axis_at] // parts).reshape((-1,) + (1,) * (len(extent) - 1 - axis_at))
    return factor_of


def routed_block(key, own, number, rows, count, top, most, slope):
    sequence = jax.random.permutation(key, count)
    crowded, usual = load_shares(count, rows * top, most, slope, True), load_shares(count, rows * top, most, slope, False)
    places = jnp.arange(count)

    def named(lengths, offset_by):
        used = int((lengths > 0).sum())
        fixed = max(1, used // 4)
        shifted = fixed + (places - fixed + offset_by * (used - fixed)) % max(1, count - fixed)
        return jnp.zeros((count,), jnp.int32).at[sequence[jnp.where(places < fixed, places, shifted)]].set(jnp.asarray(lengths, jnp.int32))

    lengths = jnp.where(number % 4 == 0, named(crowded, number // 4), named(usual, number - number // 4 - 1))
    mixed = jax.random.permutation(jax.random.fold_in(own, 3), count)
    giver, taker = mixed[0:count // 2 * 2:2], mixed[1:count // 2 * 2:2]
    slack = jnp.minimum(lengths[giver] - 1, most - lengths[taker]) // 2
    slack = jnp.where((giver == sequence[0]) | (taker == sequence[0]) | (lengths[taker] == 0), 0, jnp.maximum(slack, 0))
    shifted = jax.random.randint(jax.random.fold_in(own, 4), (count // 2,), 0, 1 << 20) % (slack + 1)
    lengths = lengths.at[giver].add(-shifted).at[taker].add(shifted)
    members = jnp.searchsorted(jnp.cumsum(lengths), jnp.arange(rows * top), side="right").astype(jnp.int32)
    listing = members.reshape(top, rows).T
    listing = listing[jax.random.permutation(jax.random.fold_in(own, 1), rows)]
    offset_by = jax.random.randint(jax.random.fold_in(own, 2), (rows, 1), 0, top)
    return jnp.take_along_axis(listing, (jnp.arange(top)[None, :] + offset_by) % top, axis=1)


def load_shares(count, total, limit, lean, full):
    portions = [(1 << 20) // math.isqrt(grade ** lean) + 1 for grade in range(1, count + 1)]
    largest = limit if full else min(limit, max(-(-total // count), total * portions[0] // sum(portions)))
    least = 1 if total - largest >= count - 1 else 0
    holding, surplus = [largest] + [least] * (count - 1), total - largest - least * (count - 1)
    while surplus > 0:
        candidates = [i for i in range(1, count) if holding[i] < largest] or [i for i in range(1, count) if holding[i] < limit]
        pool, remaining = sum([portions[i] for i in candidates]), surplus
        for i in candidates:
            addition = min(limit - holding[i], max(1, remaining * portions[i] // pool), surplus)
            holding[i] = holding[i] + addition
            surplus = surplus - addition
    return np.array(holding)


def gaussian(key, dims, scale, reach, cuts=(), held_as=jnp.bfloat16):
    values = jax.random.normal(key, dims, jnp.float32) * scale
    if len(cuts) > 0:
        values = steps_of(key, dims, cuts, -0.22, 0.18) * values
    return jnp.clip(values, min=-reach, max=reach).astype(held_as)


def setup_inputs(seed: int = 0) -> dict:
    streams_of = jax.random.split(jax.random.key(seed), 11)
    queries = gaussian(streams_of[0], (TOKEN_COUNT, HEAD_COUNT * HEAD_DIM), 0.09, 0.5, ((0, 16), (1, 8)))
    keys = gaussian(streams_of[1], (TOKEN_COUNT, HEAD_COUNT * HEAD_DIM), 0.09, 0.5, ((0, 16), (1, 8)))
    values = gaussian(streams_of[2], (TOKEN_COUNT, HEAD_COUNT * HEAD_DIM), 1.0, 6.0, ((0, 16), (1, 8)))
    attn_grad = gaussian(streams_of[3], (TOKEN_COUNT, HEAD_COUNT * HEAD_DIM), 1.0, 6.0, ((0, 16), (1, 8)))
    log_decay = draw_log_decay(jax.random.fold_in(streams_of[10], 71), 0)
    moe_grad = gaussian(streams_of[5], (TOKEN_COUNT, D), 1.0, 6.0, ((0, 16), (1, 8)))
    gate_probs = jnp.clip(0.099609375 + 0.7988281 * jax.random.uniform(streams_of[6], (TOKEN_COUNT, TOP), jnp.float32) ** steps_of(streams_of[6], (TOKEN_COUNT, TOP), ((0, 16),), -0.2, 0.2), 0.099609375, 0.8984375).astype(jnp.bfloat16)
    expert_ids_keys = jax.random.split(jax.random.fold_in(streams_of[7], 1), TOKEN_COUNT // TOK_DEV)
    expert_ids_turns = jax.random.permutation(jax.random.fold_in(streams_of[7], 3), TOKEN_COUNT // TOK_DEV)
    expert_ids = jax.vmap(lambda own, number: routed_block(jax.random.fold_in(streams_of[7], 2), own, number, TOK_DEV, EXPERTS, TOP, CAP, 1))(expert_ids_keys, expert_ids_turns).reshape((TOKEN_COUNT, TOP))
    hidden_acts = gaussian(streams_of[8], (EXPERTS, SLOTS, FF), 0.05, 0.3125, ((0, 8), (2, 16)))
    down_weight = gaussian(streams_of[9], (EXPERTS, FF, D), FF ** -0.5, 0.0625, ((0, 8), (1, 16)))
    return dict(queries=queries, keys=keys, values=values, attn_grad=attn_grad, log_decay=log_decay, moe_grad=moe_grad, gate_probs=gate_probs, expert_ids=expert_ids, hidden_acts=hidden_acts, down_weight=down_weight)


precise = lax.Precision.HIGHEST


def block_terms(query_b, key_b, value_b, grad_b, decay_b):
    cumul = jnp.cumsum(decay_b, axis=0)
    total = cumul[-1]
    tail_w = jnp.exp(total[None, :] - cumul)
    lead_w = jnp.exp(cumul)
    state_kv = jnp.einsum('th,thi,thj->hij', tail_w, key_b, value_b, precision=precise)
    state_qg = jnp.einsum('th,thi,thj->hij', lead_w, query_b, grad_b, precision=precise)
    return cumul, total, state_kv, state_qg


def block_grads(query_b, key_b, value_b, grad_b, cumul, total, incoming, upcoming):
    length = cumul.shape[0]
    causal = jnp.arange(length)[:, None] >= jnp.arange(length)[None, :]
    spread = cumul.T[:, :, None] - cumul.T[:, None, :]
    decay_mask = jnp.exp(jnp.where(causal[None], spread, -jnp.inf))
    tail_w = jnp.exp(total[None, :] - cumul)[:, :, None]
    lead_w = jnp.exp(cumul)[:, :, None]
    grad_scores = jnp.einsum('thj,shj->hts', grad_b, value_b, precision=precise) * decay_mask
    qk_scores = jnp.einsum('thi,shi->hts', query_b, key_b, precision=precise) * decay_mask
    query_g = jnp.einsum('hts,shi->thi', grad_scores, key_b, precision=precise)
    query_g = query_g + lead_w * jnp.einsum('thj,hij->thi', grad_b, incoming, precision=precise)
    key_g = jnp.einsum('hts,thi->shi', grad_scores, query_b, precision=precise)
    key_g = key_g + tail_w * jnp.einsum('shj,hij->shi', value_b, upcoming, precision=precise)
    value_g = jnp.einsum('hts,thj->shj', qk_scores, grad_b, precision=precise)
    value_g = value_g + tail_w * jnp.einsum('shi,hij->shj', key_b, upcoming, precision=precise)
    return query_g, key_g, value_g


def reference(queries, keys, values, attn_grad, log_decay, moe_grad, gate_probs, expert_ids, hidden_acts, down_weight):
    shaped = (N_SEQ, TOK_DEV, HEAD_COUNT, HEAD_DIM)
    query_f = queries.astype(jnp.float32).reshape(shaped)
    key_f = keys.astype(jnp.float32).reshape(shaped)
    value_f = values.astype(jnp.float32).reshape(shaped)
    grad_f = attn_grad.astype(jnp.float32).reshape(shaped)
    decay_f = log_decay.reshape(N_SEQ, TOK_DEV, HEAD_COUNT)
    terms = [block_terms(query_f[block], key_f[block], value_f[block], grad_f[block], decay_f[block]) for block in range(N_SEQ)]
    zero_state = jnp.zeros((HEAD_COUNT, HEAD_DIM, HEAD_DIM), jnp.float32)
    incoming = [zero_state]
    for block in range(1, N_SEQ):
        incoming.append(jnp.exp(terms[block - 1][1])[:, None, None] * incoming[-1] + terms[block - 1][2])
    upcoming = [zero_state]
    for block in range(N_SEQ - 2, -1, -1):
        upcoming.insert(0, jnp.exp(terms[block + 1][1])[:, None, None] * upcoming[0] + terms[block + 1][3])
    query_parts, key_parts, value_parts = [], [], []
    for block in range(N_SEQ):
        outs_b = block_grads(query_f[block], key_f[block], value_f[block], grad_f[block], terms[block][0], terms[block][1], incoming[block], upcoming[block])
        query_parts.append(outs_b[0].reshape(TOK_DEV, HEAD_COUNT * HEAD_DIM))
        key_parts.append(outs_b[1].reshape(TOK_DEV, HEAD_COUNT * HEAD_DIM))
        value_parts.append(outs_b[2].reshape(TOK_DEV, HEAD_COUNT * HEAD_DIM))
    query_grad = jnp.concatenate(query_parts, 0).astype(jnp.bfloat16)
    key_grad = jnp.concatenate(key_parts, 0).astype(jnp.bfloat16)
    value_grad = jnp.concatenate(value_parts, 0).astype(jnp.bfloat16)

    grad_rows = moe_grad.astype(jnp.float32)
    gate_f = gate_probs.astype(jnp.float32)
    hidden_list, weight_list = [], []
    gate_grad = jnp.zeros((TOKEN_COUNT, TOP), jnp.float32)
    for expert in range(EXPERTS):
        named = expert_ids == expert
        routed = jnp.any(named, axis=1)
        routed_int = routed.astype(jnp.int32).reshape(N_SEQ, TOK_DEV)
        slot_rank = jnp.cumsum(routed_int, axis=1) - 1
        block_base = (jnp.arange(N_SEQ, dtype=jnp.int32) * CAP)[:, None]
        slot_of = jnp.where(routed_int > 0, block_base + slot_rank, SLOTS).reshape(TOKEN_COUNT).astype(jnp.int32)
        packed = jnp.zeros((SLOTS, D), jnp.float32).at[slot_of].set(grad_rows, mode="drop")
        token_gate = jnp.sum(jnp.where(named, gate_f, 0.0), axis=1)
        slot_gate = jnp.zeros((SLOTS,), jnp.float32).at[slot_of].set(token_gate, mode="drop")
        weight_f = down_weight[expert].astype(jnp.float32)
        back_rows = jnp.dot(packed, weight_f.T, precision=precise)
        hidden_list.append((slot_gate[:, None] * back_rows).astype(jnp.bfloat16))
        hidden_f = hidden_acts[expert].astype(jnp.float32)
        slot_parts = jnp.sum(back_rows * hidden_f, axis=1)
        weighted = (slot_gate[:, None] * packed).astype(jnp.bfloat16)
        weighted_f = lax.optimization_barrier(weighted).astype(jnp.float32)
        weight_list.append(jnp.dot(hidden_f.T, weighted_f, precision=precise).astype(jnp.bfloat16))
        safe_slot = jnp.minimum(slot_of, SLOTS - 1)
        per_token = jnp.where(routed, slot_parts[safe_slot], 0.0)
        gate_grad = gate_grad + jnp.where(named, per_token[:, None], 0.0)
    hidden_grad = jnp.stack(hidden_list, 0)
    weight_grad = jnp.stack(weight_list, 0)
    return (query_grad, key_grad, value_grad, hidden_grad, weight_grad, gate_grad)
```

```python
import functools

import jax
import jax.numpy as jnp
from jax import lax
from jax.experimental import pallas as pl
from jax.experimental.pallas import tpu as pltpu
from jax.sharding import PartitionSpec as P

MESH = pl.DeviceIdType.MESH
BF, F32, I32 = jnp.bfloat16, jnp.float32, jnp.int32
NX, NY = 4, 4

OFFS = [
    (0, 0), (-1, 0), (1, 0), (0, -1), (0, 1), (2, 0), (0, 2), (-1, -1),
    (1, -1), (-1, 1), (1, 1), (2, -1), (2, 1), (-1, 2), (1, 2), (2, 2),
]
SLOT = {off: i for i, off in enumerate(OFFS)}
DIRS = {"xp": (1, 0), "xm": (-1, 0), "yp": (0, 1), "ym": (0, -1)}
H1, H2, H1b, H1a, H2a, H2b = (0, 2), (2, 4), (0, 1), (1, 2), (2, 3), (3, 4)

START = [
    ("xp", (0, 0), H1), ("xm", (0, 0), H1), ("yp", (0, 0), H2), ("ym", (0, 0), H2),
    ("xp", (0, 0), H2), ("xm", (0, 0), H2), ("yp", (0, 0), H1), ("ym", (0, 0), H1),
]
ROUND1 = [
    ([("xp", (0, 0), H1)], [("xp", (-1, 0), H1a), ("yp", (-1, 0), H1), ("ym", (-1, 0), H1)]),
    ([("xm", (0, 0), H1)], [("xm", (1, 0), H1b), ("yp", (1, 0), H1), ("ym", (1, 0), H1)]),
    ([("yp", (0, 0), H2)], [("yp", (0, -1), H2a), ("xp", (0, -1), H2), ("xm", (0, -1), H2)]),
    ([("ym", (0, 0), H2)], [("ym", (0, 1), H2b), ("xp", (0, 1), H2), ("xm", (0, 1), H2)]),
    ([("xp", (0, 0), H2)], [("xp", (-1, 0), H2a)]),
    ([("xm", (0, 0), H2)], [("xm", (1, 0), H2b)]),
    ([("yp", (0, 0), H1)], [("yp", (0, -1), H1a)]),
    ([("ym", (0, 0), H1)], [("ym", (0, 1), H1b)]),
]
ROUND2 = [
    ([("xp", (-1, 0), H1a), ("xm", (1, 0), H1b)], [("yp", (2, 0), H1), ("ym", (2, 0), H1)]),
    ([("yp", (0, -1), H2a), ("ym", (0, 1), H2b)], [("xp", (0, 2), H2), ("xm", (0, 2), H2)]),
    ([("xp", (0, -1), H2)], [("xp", (-1, -1), H2a)]),
    ([("xm", (0, -1), H2)], [("xm", (1, -1), H2b)]),
    ([("yp", (-1, 0), H1)], [("yp", (-1, -1), H1a)]),
    ([("ym", (-1, 0), H1)], [("ym", (-1, 1), H1b)]),
    ([("xp", (0, 1), H2)], [("xp", (-1, 1), H2a)]),
    ([("xm", (0, 1), H2)], [("xm", (1, 1), H2b)]),
    ([("yp", (1, 0), H1)], [("yp", (1, -1), H1a)]),
    ([("ym", (1, 0), H1)], [("ym", (1, 1), H1b)]),
    ([("xp", (-1, 0), H2a), ("xm", (1, 0), H2b), ("yp", (0, -1), H1a), ("ym", (0, 1), H1b)], []),
]
ROUND3 = [
    ([("yp", (2, 0), H1)], [("yp", (2, -1), H1a)]),
    ([("ym", (2, 0), H1)], [("ym", (2, 1), H1b)]),
    ([("xp", (0, 2), H2)], [("xp", (-1, 2), H2a)]),
    ([("xm", (0, 2), H2)], [("xm", (1, 2), H2b)]),
]
ROUND4 = [
    ([("xp", (-1, -1), H2a), ("xp", (-1, 1), H2a), ("xm", (1, -1), H2b), ("xm", (1, 1), H2b)], []),
    ([("yp", (-1, -1), H1a), ("yp", (1, -1), H1a), ("ym", (-1, 1), H1b), ("ym", (1, 1), H1b)], []),
    ([("yp", (2, -1), H1a), ("ym", (2, 1), H1b), ("xp", (-1, 2), H2a), ("xm", (1, 2), H2b)], []),
]
MSGS = START + [m for r in (ROUND1, ROUND2, ROUND3) for _, sends in r for m in sends]
INDEX = {m: i for i, m in enumerate(MSGS)}


def wrap(a, d):
    return tuple((p - q + 1) % 4 - 1 for p, q in zip(a, d))


def nn(a, b):
    return jnp.dot(a, b, preferred_element_type=F32)


def nt(a, b):
    return lax.dot_general(a, b, (((1,), (1,)), ((), ())), preferred_element_type=F32)


def iota(shape, axis):
    return lax.broadcasted_iota(I32, shape, axis)


def to_row(col, rows):
    eye = iota((rows, 128), 0) == iota((rows, 128), 1)
    return jnp.sum(jnp.where(eye, jnp.broadcast_to(col, (rows, 128)), 0.0), axis=0, keepdims=True)


def to_col(row):
    eye = iota((128, 128), 0) == iota((128, 128), 1)
    return jnp.sum(jnp.where(eye, jnp.broadcast_to(row, (128, 128)), 0.0), axis=1, keepdims=True)


def kernel(
    q_hbm, k_hbm, v_hbm, g_hbm, moe_hbm, hid_hbm, w_hbm, decay, gates, ids,
    qg_hbm, kg_hbm, vg_hbm, ho_hbm, wg_hbm, gate_out,
    qb, kb, vb, gb, moe, hid, hid_t, w, x, pack, sel, back, acc, wg, ho, parts_c,
    parts_s, parts_r, tok_s, tok_r, st_s, st_r, res_s, res_r, cum, qo, ko, vo,
    load_sem, out_sem, z_send, z_recv, a_send, a_recv, b_send, b_recv,
    x_send, x_recv, p_send, p_recv, t_send, t_recv,
):
    n_seq, n_exp = lax.axis_size("seq"), lax.axis_size("exp")
    me, e = lax.axis_index("seq"), lax.axis_index("exp")
    my_y, my_x = me // NX, me % NX
    cap = x.shape[0] // n_seq
    feat = moe.shape[1]
    width = w.shape[1]
    heads = decay.shape[1]
    quarter = width // 4

    def seq_at(off):
        return ((my_y + off[1] + NY) % NY) * NX + (my_x + off[0] + NX) % NX

    def remote(src, dst, ss, rs, where):
        return pltpu.make_async_remote_copy(
            src_ref=src, dst_ref=dst, send_sem=ss, recv_sem=rs,
            device_id=where, device_id_type=MESH,
        )

    loads = [(moe_hbm, moe), (q_hbm, qb), (k_hbm, kb), (v_hbm, vb), (g_hbm, gb)]
    loads = [pltpu.make_async_copy(a, b, load_sem.at[i]) for i, (a, b) in enumerate(loads)]
    n_load = len(loads)
    hid_loads = []
    for i, off in enumerate(OFFS):
        start = pl.multiple_of(seq_at(off) * cap, 16)
        hid_loads.append(pltpu.make_async_copy(
            hid_hbm.at[pl.ds(start, cap)], hid.at[pl.ds(i * cap, cap)], load_sem.at[n_load + i]))
    w_load = pltpu.make_async_copy(w_hbm, w, load_sem.at[n_load + n_seq])
    for c in loads + hid_loads + [w_load]:
        c.start()

    barrier = pltpu.get_barrier_semaphore()
    for off in range(1, n_seq):
        pl.semaphore_signal(barrier, inc=1, device_id={"seq": (me + off) % n_seq}, device_id_type=MESH)
    for off in range(1, n_exp):
        pl.semaphore_signal(barrier, inc=1, device_id={"exp": (e + off) % n_exp}, device_id_type=MESH)

    ids_f = ids[...].astype(F32)
    gates_f = gates[...].astype(F32)
    e_f = e.astype(F32)
    id_rows = [to_row(ids_f[:, k:k + 1], 128) for k in range(2)]
    expert = iota((n_exp, 128), 0).astype(F32)
    routed = jnp.where((expert == id_rows[0]) | (expert == id_rows[1]), 1.0, 0.0)
    upto = jnp.where(iota((128, 128), 0) <= iota((128, 128), 1), 1.0, 0.0).astype(BF)
    rank = nn(routed.astype(BF), upto) - 1.0
    rank = jnp.where(routed > 0.0, rank, -1.0)
    slot_no = iota((cap, 128), 0).astype(F32)
    loads[0].wait()
    for i in range(n_exp):
        chosen = jnp.where(rank[i:i + 1, :] == slot_no, 1.0, 0.0)
        pack[pl.ds(i * cap, cap), :] = nn(chosen.astype(BF), moe[...]).astype(BF)
    own_rank = jnp.max(jnp.where(expert == e_f, rank, -1.0), axis=0, keepdims=True)
    own = jnp.where(own_rank == slot_no, 1.0, 0.0)
    sel[...] = own
    tok_gate = sum(jnp.where(ids_f[:, k:k + 1] == e_f, gates_f[:, k:k + 1], 0.0) for k in range(2))
    slot_gate = jnp.sum(own * to_row(tok_gate, 128), axis=1, keepdims=True)
    x[0:cap, width:] = jnp.broadcast_to(slot_gate, (cap, 128)).astype(BF)

    pl.semaphore_wait(barrier, n_seq - 1 + n_exp - 1)

    col_here = pl.ds(pl.multiple_of(e * feat, 128), feat)
    z_copies = []
    for off in range(1, n_exp):
        peer = (e + off) % n_exp
        z_copies.append(remote(
            pack.at[pl.ds(pl.multiple_of(peer * cap, 16), cap)], x.at[pl.ds(0, cap), col_here],
            z_send.at[off], z_recv.at[off], {"exp": peer}))
        z_copies[-1].start()
    x[0:cap, col_here] = pack[pl.ds(pl.multiple_of(e * cap, 16), cap), :]

    cum[...] = jnp.dot(
        jnp.where(iota((128, 128), 0) >= iota((128, 128), 1), 1.0, 0.0), decay[...],
        preferred_element_type=F32, precision=lax.Precision.HIGHEST)
    for c in loads[1:]:
        c.wait()

    def head_terms(h):
        here = iota((128, heads), 1) == h
        col = jnp.sum(jnp.where(here, cum[...], 0.0), axis=1, keepdims=True)
        return col, col[127:128, :]

    def local_state(h, carry):
        col, total = head_terms(h)
        cols = pl.ds(pl.multiple_of(h * 128, 128), 128)
        kw = (kb[:, cols].astype(F32) * jnp.exp(total - col)).T.astype(BF)
        qw = (qb[:, cols].astype(F32) * jnp.exp(col)).T.astype(BF)
        kv = nn(kw, vb[:, cols]).astype(BF)
        qg = nn(qw, gb[:, cols]).astype(BF)
        gain = jnp.broadcast_to(jnp.exp(total), (16, 128))
        hi = gain.astype(BF).astype(F32)
        mid = (gain - hi).astype(BF).astype(F32)
        low = gain - hi - mid
        row = iota((16, 128), 0)
        three = jnp.where(row == 0, hi, jnp.where(row == 1, mid, jnp.where(row == 2, low, 0.0))).astype(BF)
        for p in range(2):
            st_s[2 * h + p, 0:64, :] = kv[64 * p:64 * p + 64, :]
            st_s[2 * h + p, 64:128, :] = qg[64 * p:64 * p + 64, :]
            st_s[2 * h + p, 128:144, :] = three
        return carry

    lax.fori_loop(0, heads, local_state, 0)
    a_copies = []
    for off in range(1, n_seq):
        peer = (me + off) % n_seq
        a_copies.append(remote(st_s.at[peer], st_r.at[me], a_send.at[off], a_recv.at[off], {"seq": peer}))
        a_copies[-1].start()
    st_r[me] = st_s[me]

    def span(q):
        stop = width + 128 if q[1] == 4 else q[1] * quarter
        return pl.ds(q[0] * quarter, stop - q[0] * quarter)

    def message(m):
        d, off, q = m
        i = INDEX[m]
        src = x.at[pl.ds(SLOT[off] * cap, cap), span(q)]
        dst = x.at[pl.ds(SLOT[wrap(off, DIRS[d])] * cap, cap), span(q)]
        return remote(src, dst, x_send.at[i], x_recv.at[i], {"seq": seq_at(DIRS[d])})

    def go(steps):
        for waits, sends in steps:
            for m in waits:
                message(m).wait_recv()
            for m in sends:
                message(m).start()

    for c in z_copies:
        c.wait_recv()
    go([([], START)])

    for c in a_copies:
        c.wait_recv()

    def gain_of(b):
        g3 = st_r[b, 128:144, :].astype(F32)
        return g3[0:1, :] + g3[1:2, :] + g3[2:3, :]

    def scan_up(b, state):
        res_s[b, 0:64, :] = state.astype(BF)
        return gain_of(b) * state + st_r[b, 0:64, :].astype(F32)

    def scan_down(i, state):
        b = n_seq - 1 - i
        res_s[b, 64:128, :] = state.astype(BF)
        return gain_of(b) * state + st_r[b, 64:128, :].astype(F32)

    zero = jnp.zeros((64, 128), F32)
    lax.fori_loop(0, n_seq, scan_up, zero)
    lax.fori_loop(0, n_seq, scan_down, zero)
    b_copies = []
    for off in range(1, n_seq):
        peer = (me + off) % n_seq
        b_copies.append(remote(res_s.at[peer], res_r.at[me], b_send.at[off], b_recv.at[off], {"seq": peer}))
        b_copies[-1].start()
    res_r[me] = res_s[me]

    for c in hid_loads:
        c.wait()

    def turn(i, carry):
        rows = pl.ds(pl.multiple_of(i * 128, 128), 128)
        hid_t[:, rows] = hid[rows, :].astype(F32).T.astype(BF)
        return carry

    lax.fori_loop(0, hid.shape[0] // 128, turn, 0)

    go(ROUND1)

    for c in b_copies:
        c.wait_recv()

    def finish_head(h, carry):
        col, total = head_terms(h)
        cols = pl.ds(pl.multiple_of(h * 128, 128), 128)
        q, k, v, g = qb[:, cols], kb[:, cols], vb[:, cols], gb[:, cols]
        two = res_r[pl.ds(2 * h, 2)]
        inc = two[:, 0:64, :].reshape(128, 128)
        upc = two[:, 64:128, :].reshape(128, 128)
        lead, tail = jnp.exp(col), jnp.exp(total - col)
        spread = jnp.broadcast_to(col, (128, 128)) - to_row(col, 128)
        causal = iota((128, 128), 0) >= iota((128, 128), 1)
        mask = jnp.exp(jnp.where(causal, spread, -jnp.inf))
        gs = nt(g, v) * mask
        qk = nt(q, k) * mask
        qo[:, cols] = (nn(gs.astype(BF), k) + lead * nt(g, inc)).astype(BF)
        ko[:, cols] = (nn(gs.T.astype(BF), q) + tail * nt(v, upc)).astype(BF)
        vo[:, cols] = (nn(qk.T.astype(BF), g) + tail * nn(k, upc)).astype(BF)
        return carry

    lax.fori_loop(0, heads, finish_head, 0)
    outs = [(qo, qg_hbm), (ko, kg_hbm), (vo, vg_hbm)]
    outs = [pltpu.make_async_copy(a, b, out_sem.at[i]) for i, (a, b) in enumerate(outs)]
    for c in outs:
        c.start()

    go(ROUND2)

    chunk = 512
    chunks = width // chunk
    n_rows = x.shape[0]
    cut = 512

    def product(start, count):
        rows = pl.ds(start, count)
        back[rows, :] = jnp.zeros((count, back.shape[1]), F32)

        def one(i, carry):
            cols = pl.ds(pl.multiple_of(i * chunk, chunk), chunk)
            back[rows, :] += nt(x[rows, cols], w[:, cols])
            return carry

        lax.fori_loop(0, chunks, one, 0)

        def after(i, carry):
            part = pl.ds(pl.multiple_of(start + i * 64, 64), 64)
            b = back[part, :]
            gate = x[part, width:][:, 0:1].astype(F32)
            ho[part, :] = (gate * b).astype(BF)
            total = jnp.sum(b * hid[part, :].astype(F32), axis=1, keepdims=True)
            parts_c[part, :] = jnp.broadcast_to(total, (64, 128))
            return carry

        lax.fori_loop(0, count // 64, after, 0)

    def scaled(start, count, cols):
        rows = pl.ds(start, count)
        gate = x[rows, width:]
        return x[rows, cols] * jnp.concatenate([gate] * (chunk // 128), axis=1)

    p_copies, ho_copies = [], []

    def hand_out(first, last):
        for i in range(first, last):
            rows = pl.ds(i * cap, cap)
            parts_s[i] = jnp.broadcast_to(to_row(parts_c[rows, :][:, 0:1], cap), (8, 128))
            owner = seq_at(OFFS[i])
            c = pltpu.make_async_copy(
                ho.at[rows], ho_hbm.at[pl.ds(pl.multiple_of(owner * cap, 16), cap)], out_sem.at[3 + i])
            c.start()
            ho_copies.append(c)
            if i > 0:
                c = remote(parts_s.at[i], parts_r.at[i], p_send.at[i], p_recv.at[i], {"seq": owner})
                c.start()
                p_copies.append(c)

    w_load.wait()
    product(0, cut)
    go(ROUND3)
    hand_out(0, cut // cap)

    def first_grad(i, carry):
        cols = pl.ds(pl.multiple_of(i * chunk, chunk), chunk)
        acc[:, cols] = nn(hid_t[:, 0:cut], scaled(0, cut, cols))
        return carry

    lax.fori_loop(0, chunks, first_grad, 0)
    go(ROUND4)
    product(cut, n_rows - cut)
    hand_out(cut // cap, n_seq)

    def wg_copy(i):
        cols = pl.ds(pl.multiple_of(i * chunk, chunk), chunk)
        return pltpu.make_async_copy(wg.at[:, cols], wg_hbm.at[:, cols], out_sem.at[3 + n_seq + i])

    def last_grad(i, carry):
        cols = pl.ds(pl.multiple_of(i * chunk, chunk), chunk)
        wg[:, cols] = (acc[:, cols] + nn(hid_t[:, cut:], scaled(cut, n_rows - cut, cols))).astype(BF)
        wg_copy(i).start()
        return carry

    lax.fori_loop(0, chunks, last_grad, 0)

    total = parts_s[0]
    for i, c in enumerate(p_copies):
        c.wait_recv()
        total = total + parts_r[i + 1]
    per_tok = jnp.sum(sel[...] * to_col(total[0:1, :])[0:cap, :], axis=0, keepdims=True)
    tok_s[...] = jnp.broadcast_to(per_tok, (8, 128))
    t_copies = []
    for off in range(1, n_exp):
        peer = (e + off) % n_exp
        t_copies.append(remote(tok_s, tok_r.at[e], t_send.at[off], t_recv.at[off], {"exp": peer}))
        t_copies[-1].start()
    tok_r[e] = tok_s[...]
    for c in t_copies:
        c.wait_recv()
    by_expert = [to_col(tok_r[i, 0:1, :]) for i in range(n_exp)]
    result = []
    for k in range(2):
        result.append(sum(jnp.where(ids_f[:, k:k + 1] == float(i), by_expert[i], 0.0) for i in range(n_exp)))
    gate_out[...] = jnp.where(iota((128, 2), 1) == 0, result[0], result[1])

    for c in z_copies + a_copies + b_copies + p_copies + t_copies:
        c.wait_send()
    for m in MSGS:
        message(m).wait_send()
    for c in outs + ho_copies:
        c.wait()
    for i in range(chunks):
        wg_copy(i).wait()


def on_device(
    queries, keys, values, attn_grad, log_decay, moe_grad, gate_probs, expert_ids, hidden_acts, down_weight
):
    n_seq, n_exp = lax.axis_size("seq"), lax.axis_size("exp")
    _, slots, units = hidden_acts.shape
    width = down_weight.shape[2]
    toks, flat = queries.shape
    feat = moe_grad.shape[1]
    hbm = pl.BlockSpec(memory_space=pl.ANY)
    vmem = pl.BlockSpec(memory_space=pltpu.VMEM)
    dma = pltpu.SemaphoreType.DMA
    V = pltpu.VMEM
    wide = V((toks, flat), BF)
    out = pl.pallas_call(
        kernel,
        out_shape=(
            jax.ShapeDtypeStruct((toks, flat), BF),
            jax.ShapeDtypeStruct((toks, flat), BF),
            jax.ShapeDtypeStruct((toks, flat), BF),
            jax.ShapeDtypeStruct((slots, units), BF),
            jax.ShapeDtypeStruct((units, width), BF),
            jax.ShapeDtypeStruct(gate_probs.shape, F32),
        ),
        in_specs=[hbm] * 7 + [vmem] * 3,
        out_specs=(hbm,) * 5 + (vmem,),
        scratch_shapes=[
            wide, wide, wide, wide, V((toks, feat), BF),
            V((slots, units), BF), V((units, slots), BF), V((units, width), BF),
            V((slots, width + 128), BF), V((n_exp * slots // n_seq, feat), BF),
            V((slots // n_seq, 128), F32), V((slots, units), F32), V((units, width), F32),
            V((units, width), BF), V((slots, units), BF), V((slots, 128), F32),
            V((n_seq, 8, 128), F32), V((n_seq, 8, 128), F32),
            V((8, 128), F32), V((n_exp, 8, 128), F32),
            V((n_seq, 144, 128), BF), V((n_seq, 144, 128), BF),
            V((n_seq, 128, 128), BF), V((n_seq, 128, 128), BF),
            V(log_decay.shape, F32), wide, wide, wide,
            dma((5 + n_seq + 1,)), dma((3 + n_seq + width // 512,)),
            dma((n_exp,)), dma((n_exp,)), dma((n_seq,)), dma((n_seq,)), dma((n_seq,)), dma((n_seq,)),
            dma((len(MSGS),)), dma((len(MSGS),)), dma((n_seq,)), dma((n_seq,)), dma((n_exp,)), dma((n_exp,)),
        ],
        compiler_params=pltpu.CompilerParams(
            collective_id=0, has_side_effects=True, vmem_limit_bytes=60 * 1024 * 1024
        ),
    )(
        queries, keys, values, attn_grad, moe_grad, hidden_acts[0], down_weight[0],
        log_decay, gate_probs, expert_ids,
    )
    return (*out[:3], out[3][None], out[4][None], out[5])


def solution(mesh):
    return jax.shard_map(
        on_device,
        mesh=mesh,
        in_specs=(
            P("seq", "exp"),
            P("seq", "exp"),
            P("seq", "exp"),
            P("seq", "exp"),
            P("seq", "exp"),
            P("seq", "exp"),
            P("seq", None),
            P("seq", None),
            P("exp", None, "seq"),
            P("exp", "seq", None),
        ),
        out_specs=(
            P("seq", "exp"),
            P("seq", "exp"),
            P("seq", "exp"),
            P("exp", None, "seq"),
            P("exp", "seq", None),
            P("seq", None),
        ),
        check_vma=False,
    )
```

```python
import functools

import jax
import jax.numpy as jnp
from jax import lax
from jax.experimental import pallas as pl
from jax.experimental.pallas import tpu as pltpu
from jax.sharding import PartitionSpec as P

MESH = pl.DeviceIdType.MESH
BF, F32, I32 = jnp.bfloat16, jnp.float32, jnp.int32
NX, NY = 4, 4

OFFS = [
    (0, 0), (-1, 0), (1, 0), (0, -1), (0, 1), (2, 0), (0, 2), (-1, -1),
    (1, -1), (-1, 1), (1, 1), (2, -1), (2, 1), (-1, 2), (1, 2), (2, 2),
]
SLOT = {off: i for i, off in enumerate(OFFS)}
DIRS = {"xp": (1, 0), "xm": (-1, 0), "yp": (0, 1), "ym": (0, -1)}
H1, H2, H1b, H1a, H2a, H2b = (0, 2), (2, 4), (0, 1), (1, 2), (2, 3), (3, 4)

START = [
    ("xp", (0, 0), H1), ("xm", (0, 0), H1), ("yp", (0, 0), H2), ("ym", (0, 0), H2),
    ("xp", (0, 0), H2), ("xm", (0, 0), H2), ("yp", (0, 0), H1), ("ym", (0, 0), H1),
]
ROUND1 = [
    ([("xp", (0, 0), H1)], [("xp", (-1, 0), H1a), ("yp", (-1, 0), H1), ("ym", (-1, 0), H1)]),
    ([("xm", (0, 0), H1)], [("xm", (1, 0), H1b), ("yp", (1, 0), H1), ("ym", (1, 0), H1)]),
    ([("yp", (0, 0), H2)], [("yp", (0, -1), H2a), ("xp", (0, -1), H2), ("xm", (0, -1), H2)]),
    ([("ym", (0, 0), H2)], [("ym", (0, 1), H2b), ("xp", (0, 1), H2), ("xm", (0, 1), H2)]),
    ([("xp", (0, 0), H2)], [("xp", (-1, 0), H2a)]),
    ([("xm", (0, 0), H2)], [("xm", (1, 0), H2b)]),
    ([("yp", (0, 0), H1)], [("yp", (0, -1), H1a)]),
    ([("ym", (0, 0), H1)], [("ym", (0, 1), H1b)]),
]
ROUND2 = [
    ([("xp", (-1, 0), H1a), ("xm", (1, 0), H1b)], [("yp", (2, 0), H1), ("ym", (2, 0), H1)]),
    ([("yp", (0, -1), H2a), ("ym", (0, 1), H2b)], [("xp", (0, 2), H2), ("xm", (0, 2), H2)]),
    ([("xp", (0, -1), H2)], [("xp", (-1, -1), H2a)]),
    ([("xm", (0, -1), H2)], [("xm", (1, -1), H2b)]),
    ([("yp", (-1, 0), H1)], [("yp", (-1, -1), H1a)]),
    ([("ym", (-1, 0), H1)], [("ym", (-1, 1), H1b)]),
    ([("xp", (0, 1), H2)], [("xp", (-1, 1), H2a)]),
    ([("xm", (0, 1), H2)], [("xm", (1, 1), H2b)]),
    ([("yp", (1, 0), H1)], [("yp", (1, -1), H1a)]),
    ([("ym", (1, 0), H1)], [("ym", (1, 1), H1b)]),
    ([("xp", (-1, 0), H2a), ("xm", (1, 0), H2b), ("yp", (0, -1), H1a), ("ym", (0, 1), H1b)], []),
]
ROUND3 = [
    ([("yp", (2, 0), H1)], [("yp", (2, -1), H1a)]),
    ([("ym", (2, 0), H1)], [("ym", (2, 1), H1b)]),
    ([("xp", (0, 2), H2)], [("xp", (-1, 2), H2a)]),
    ([("xm", (0, 2), H2)], [("xm", (1, 2), H2b)]),
]
ROUND4 = [
    ([("xp", (-1, -1), H2a), ("xp", (-1, 1), H2a), ("xm", (1, -1), H2b), ("xm", (1, 1), H2b)], []),
    ([("yp", (-1, -1), H1a), ("yp", (1, -1), H1a), ("ym", (-1, 1), H1b), ("ym", (1, 1), H1b)], []),
    ([("yp", (2, -1), H1a), ("ym", (2, 1), H1b), ("xp", (-1, 2), H2a), ("xm", (1, 2), H2b)], []),
]
MSGS = START + [m for r in (ROUND1, ROUND2, ROUND3) for _, sends in r for m in sends]
INDEX = {m: i for i, m in enumerate(MSGS)}


def wrap(a, d):
    return tuple((p - q + 1) % 4 - 1 for p, q in zip(a, d))


def nn(a, b):
    return jnp.dot(a, b, preferred_element_type=F32)


def nt(a, b):
    return lax.dot_general(a, b, (((1,), (1,)), ((), ())), preferred_element_type=F32)


def iota(shape, axis):
    return lax.broadcasted_iota(I32, shape, axis)


def to_row(col, rows):
    eye = iota((rows, 128), 0) == iota((rows, 128), 1)
    return jnp.sum(jnp.where(eye, jnp.broadcast_to(col, (rows, 128)), 0.0), axis=0, keepdims=True)


def to_col(row):
    eye = iota((128, 128), 0) == iota((128, 128), 1)
    return jnp.sum(jnp.where(eye, jnp.broadcast_to(row, (128, 128)), 0.0), axis=1, keepdims=True)


def kernel(
    q_hbm, k_hbm, v_hbm, g_hbm, moe_hbm, hid_hbm, w_hbm, decay, gates, ids,
    qo, ko, vo, ho_out, wg, gate_out,
    qb, kb, vb, gb, moe, hid, hid_t, order, w, x, pack, sel, back, acc, ho, parts,
    parts_s, parts_r, tok_s, tok_r, st_s, st_r, res_s, res_r, cum,
    load_sem, z_send, z_recv, a_send, a_recv, b_send, b_recv,
    x_send, x_recv, p_send, p_recv, t_send, t_recv,
):
    n_seq, n_exp = lax.axis_size("seq"), lax.axis_size("exp")
    me, e = lax.axis_index("seq"), lax.axis_index("exp")
    my_y, my_x = me // NX, me % NX
    cap = x.shape[0] // n_seq
    feat = moe.shape[1]
    width = w.shape[1]
    heads = decay.shape[0]
    quarter = width // 4

    def seq_at(off):
        return ((my_y + off[1] + NY) % NY) * NX + (my_x + off[0] + NX) % NX

    def remote(src, dst, ss, rs, where):
        return pltpu.make_async_remote_copy(
            src_ref=src, dst_ref=dst, send_sem=ss, recv_sem=rs,
            device_id=where, device_id_type=MESH,
        )

    loads = [
        (moe_hbm, moe), (q_hbm, qb), (k_hbm, kb), (v_hbm, vb), (g_hbm, gb), (hid_hbm, hid), (w_hbm, w)
    ]
    loads = [pltpu.make_async_copy(a, b, load_sem.at[i]) for i, (a, b) in enumerate(loads)]
    for c in loads:
        c.start()

    barrier = pltpu.get_barrier_semaphore()
    for off in range(1, n_seq):
        pl.semaphore_signal(barrier, inc=1, device_id={"seq": (me + off) % n_seq}, device_id_type=MESH)
    for off in range(1, n_exp):
        pl.semaphore_signal(barrier, inc=1, device_id={"exp": (e + off) % n_exp}, device_id_type=MESH)

    ids_f = ids[...].astype(F32)
    gates_f = gates[...].astype(F32)
    e_f = e.astype(F32)
    id_rows = [ids_f[k:k + 1, :] for k in range(2)]
    expert = iota((n_exp, 128), 0).astype(F32)
    routed = jnp.where((expert == id_rows[0]) | (expert == id_rows[1]), 1.0, 0.0)
    upto = jnp.where(iota((128, 128), 0) <= iota((128, 128), 1), 1.0, 0.0).astype(BF)
    rank = nn(routed.astype(BF), upto) - 1.0
    rank = jnp.where(routed > 0.0, rank, -1.0)
    slot_no = iota((cap, 128), 0).astype(F32)
    loads[0].wait()
    for i in range(n_exp):
        chosen = jnp.where(rank[i:i + 1, :] == slot_no, 1.0, 0.0)
        pack[pl.ds(i * cap, cap), :] = nn(chosen.astype(BF), moe[...]).astype(BF)
    own_rank = jnp.max(jnp.where(expert == e_f, rank, -1.0), axis=0, keepdims=True)
    own = jnp.where(own_rank == slot_no, 1.0, 0.0)
    sel[...] = own
    tok_gate = sum(jnp.where(id_rows[k] == e_f, gates_f[k:k + 1, :], 0.0) for k in range(2))
    slot_gate = jnp.sum(own * tok_gate, axis=1, keepdims=True)
    x[0:cap, width:] = jnp.broadcast_to(slot_gate, (cap, 128)).astype(BF)

    pl.semaphore_wait(barrier, n_seq - 1 + n_exp - 1)

    col_here = pl.ds(pl.multiple_of(e * feat, 128), feat)
    z_copies = []
    for off in range(1, n_exp):
        peer = (e + off) % n_exp
        z_copies.append(remote(
            pack.at[pl.ds(pl.multiple_of(peer * cap, 16), cap)], x.at[pl.ds(0, cap), col_here],
            z_send.at[off], z_recv.at[off], {"exp": peer}))
        z_copies[-1].start()
    x[0:cap, col_here] = pack[pl.ds(pl.multiple_of(e * cap, 16), cap), :]

    cum[...] = jnp.dot(
        decay[...], jnp.where(iota((128, 128), 0) <= iota((128, 128), 1), 1.0, 0.0),
        preferred_element_type=F32, precision=lax.Precision.HIGHEST)
    for c in loads[1:5]:
        c.wait()

    def head_terms(h):
        row = jnp.sum(jnp.where(iota((heads, 128), 0) == h, cum[...], 0.0), axis=0, keepdims=True)
        col = to_col(row)
        return row, col, col[127:128, :]

    def local_state(h, carry):
        row, col, total = head_terms(h)
        cols = pl.ds(pl.multiple_of(h * 128, 128), 128)
        kw = (kb[:, cols].astype(F32) * jnp.exp(total - col)).T.astype(BF)
        qw = (qb[:, cols].astype(F32) * jnp.exp(col)).T.astype(BF)
        kv = nn(kw, vb[:, cols]).astype(BF)
        qg = nn(qw, gb[:, cols]).astype(BF)
        gain = jnp.broadcast_to(jnp.exp(total), (16, 128))
        hi = gain.astype(BF).astype(F32)
        mid = (gain - hi).astype(BF).astype(F32)
        low = gain - hi - mid
        line = iota((16, 128), 0)
        three = jnp.where(line == 0, hi, jnp.where(line == 1, mid, jnp.where(line == 2, low, 0.0))).astype(BF)
        for p in range(2):
            st_s[2 * h + p, 0:64, :] = kv[64 * p:64 * p + 64, :]
            st_s[2 * h + p, 64:128, :] = qg[64 * p:64 * p + 64, :]
            st_s[2 * h + p, 128:144, :] = three
        return carry

    lax.fori_loop(0, heads, local_state, 0)
    a_copies = []
    for off in range(1, n_seq):
        peer = (me + off) % n_seq
        a_copies.append(remote(st_s.at[peer], st_r.at[me], a_send.at[off], a_recv.at[off], {"seq": peer}))
        a_copies[-1].start()
    st_r[me] = st_s[me]

    def span(q):
        stop = width + 128 if q[1] == 4 else q[1] * quarter
        return pl.ds(q[0] * quarter, stop - q[0] * quarter)

    def message(m):
        d, off, q = m
        i = INDEX[m]
        src = x.at[pl.ds(SLOT[off] * cap, cap), span(q)]
        dst = x.at[pl.ds(SLOT[wrap(off, DIRS[d])] * cap, cap), span(q)]
        return remote(src, dst, x_send.at[i], x_recv.at[i], {"seq": seq_at(DIRS[d])})

    def go(steps):
        for waits, sends in steps:
            for m in waits:
                message(m).wait_recv()
            for m in sends:
                message(m).start()

    for c in z_copies:
        c.wait_recv()
    go([([], START)])

    for c in a_copies:
        c.wait_recv()

    def gain_of(b):
        g3 = st_r[b, 128:144, :].astype(F32)
        return g3[0:1, :] + g3[1:2, :] + g3[2:3, :]

    def scan_up(b, state):
        res_s[b, 0:64, :] = state.astype(BF)
        return gain_of(b) * state + st_r[b, 0:64, :].astype(F32)

    def scan_down(i, state):
        b = n_seq - 1 - i
        res_s[b, 64:128, :] = state.astype(BF)
        return gain_of(b) * state + st_r[b, 64:128, :].astype(F32)

    zero = jnp.zeros((64, 128), F32)
    lax.fori_loop(0, n_seq, scan_up, zero)
    lax.fori_loop(0, n_seq, scan_down, zero)
    b_copies = []
    for off in range(1, n_seq):
        peer = (me + off) % n_seq
        b_copies.append(remote(res_s.at[peer], res_r.at[me], b_send.at[off], b_recv.at[off], {"seq": peer}))
        b_copies[-1].start()
    res_r[me] = res_s[me]

    n_rows = x.shape[0]
    place = iota((1, n_rows), 1)
    source = place
    for i, off in enumerate(OFFS):
        inside = (place >= i * cap) & (place < (i + 1) * cap)
        source = source + jnp.where(inside, (seq_at(off) - i) * cap, 0)

    def make_order(i, carry):
        first = pl.multiple_of(i * 64, 64)
        hit = iota((64, n_rows), 0) + first == source
        order[pl.ds(first, 64), :] = jnp.where(hit, 1.0, 0.0).astype(BF)
        return carry

    lax.fori_loop(0, n_rows // 64, make_order, 0)
    loads[5].wait()
    hid_t[...] = nn(hid[...], order[...]).astype(BF)

    go(ROUND1)

    for c in b_copies:
        c.wait_recv()

    def finish_head(h, carry):
        row, col, total = head_terms(h)
        cols = pl.ds(pl.multiple_of(h * 128, 128), 128)
        q, k, v, g = qb[:, cols], kb[:, cols], vb[:, cols], gb[:, cols]
        two = res_r[pl.ds(2 * h, 2)]
        inc = two[:, 0:64, :].reshape(128, 128)
        upc = two[:, 64:128, :].reshape(128, 128)
        lead, tail = jnp.exp(col), jnp.exp(total - col)
        spread = jnp.broadcast_to(col, (128, 128)) - jnp.broadcast_to(row, (128, 128))
        causal = iota((128, 128), 0) >= iota((128, 128), 1)
        mask = jnp.exp(jnp.where(causal, spread, -jnp.inf))
        gs = nt(g, v) * mask
        qk = nt(q, k) * mask
        qo[:, cols] = (nn(gs.astype(BF), k) + lead * nt(g, inc)).astype(BF)
        ko[:, cols] = (nn(gs.T.astype(BF), q) + tail * nt(v, upc)).astype(BF)
        vo[:, cols] = (nn(qk.T.astype(BF), g) + tail * nn(k, upc)).astype(BF)
        return carry

    lax.fori_loop(0, heads, finish_head, 0)
    go(ROUND2)

    chunk = 512
    chunks = width // chunk
    cut = 512
    units = w.shape[0]

    def product(start, count):
        rows = pl.ds(start, count)
        back[:, rows] = jnp.zeros((units, count), F32)

        def one(i, carry):
            cols = pl.ds(pl.multiple_of(i * chunk, chunk), chunk)
            back[:, rows] += nt(w[:, cols], x[rows, cols])
            return carry

        lax.fori_loop(0, chunks, one, 0)
        first = jnp.where(iota((8, 128), 1) == 0, 1.0, 0.0).astype(BF)
        gate = nt(first, x[rows, width:])[0:1, :]

        def after(i, total):
            part = pl.ds(pl.multiple_of(i * 64, 64), 64)
            b = back[part, rows]
            ho[part, rows] = (gate * b).astype(BF)
            return total + jnp.sum(b * hid_t[part, rows].astype(F32), axis=0, keepdims=True)

        total = lax.fori_loop(0, units // 64, after, jnp.zeros((1, count), F32))
        parts[0:1, rows] = total

    def scaled(start, count, cols):
        rows = pl.ds(start, count)
        gate = x[rows, width:]
        return x[rows, cols] * jnp.concatenate([gate] * (chunk // 128), axis=1)

    p_copies = []
    parts_s[...] = jnp.zeros_like(parts_s)

    def hand_out(first, last):
        for i in range(first, last):
            parts_s[i, 0:1, 0:cap] = parts[0:1, i * cap:(i + 1) * cap]
            if i > 0:
                owner = {"seq": seq_at(OFFS[i])}
                c = remote(parts_s.at[i], parts_r.at[i], p_send.at[i], p_recv.at[i], owner)
                c.start()
                p_copies.append(c)

    loads[6].wait()
    product(0, cut)
    go(ROUND3)
    hand_out(0, cut // cap)

    def first_grad(i, carry):
        cols = pl.ds(pl.multiple_of(i * chunk, chunk), chunk)
        acc[:, cols] = nn(hid_t[:, 0:cut], scaled(0, cut, cols))
        return carry

    lax.fori_loop(0, chunks, first_grad, 0)
    go(ROUND4)
    product(cut, n_rows - cut)
    hand_out(cut // cap, n_seq)

    def last_grad(i, carry):
        cols = pl.ds(pl.multiple_of(i * chunk, chunk), chunk)
        wg[:, cols] = (acc[:, cols] + nn(hid_t[:, cut:], scaled(cut, n_rows - cut, cols))).astype(BF)
        return carry

    lax.fori_loop(0, chunks, last_grad, 0)
    ho_out[...] = nt(ho[...], order[...]).astype(BF)

    total = parts_s[0]
    for i, c in enumerate(p_copies):
        c.wait_recv()
        total = total + parts_r[i + 1]
    per_tok = jnp.sum(sel[...] * to_col(total[0:1, :])[0:cap, :], axis=0, keepdims=True)
    tok_s[...] = jnp.broadcast_to(per_tok, (8, 128))
    t_copies = []
    for off in range(1, n_exp):
        peer = (e + off) % n_exp
        t_copies.append(remote(tok_s, tok_r.at[e], t_send.at[off], t_recv.at[off], {"exp": peer}))
        t_copies[-1].start()
    tok_r[e] = tok_s[...]
    for c in t_copies:
        c.wait_recv()
    for k in range(2):
        gate_out[k:k + 1, :] = sum(
            jnp.where(id_rows[k] == float(i), tok_r[i, 0:1, :], 0.0) for i in range(n_exp))

    for c in z_copies + a_copies + b_copies + p_copies + t_copies:
        c.wait_send()
    for m in MSGS:
        message(m).wait_send()


def write_out(*refs):
    n = (len(refs) - 1) // 2
    copies = [pltpu.make_async_copy(a, b, refs[-1].at[i]) for i, (a, b) in enumerate(zip(refs[:n], refs[n:-1]))]
    for c in copies:
        c.start()
    for c in copies:
        c.wait()


def on_device(
    queries, keys, values, attn_grad, log_decay, moe_grad, gate_probs, expert_ids, hidden_acts, down_weight
):
    n_seq, n_exp = lax.axis_size("seq"), lax.axis_size("exp")
    _, slots, units = hidden_acts.shape
    width = down_weight.shape[2]
    toks, flat = queries.shape
    feat = moe_grad.shape[1]
    hbm = pl.BlockSpec(memory_space=pl.ANY)
    vmem = pl.BlockSpec(memory_space=pltpu.VMEM)
    dma = pltpu.SemaphoreType.DMA
    V = pltpu.VMEM
    wide = V((toks, flat), BF)
    shapes = [
        ((toks, flat), BF), ((toks, flat), BF), ((toks, flat), BF),
        ((units, slots), BF), ((units, width), BF), ((2, toks), F32),
    ]
    held = pl.pallas_call(
        kernel,
        out_shape=tuple(V(*s) for s in shapes),
        in_specs=[hbm] * 7 + [vmem] * 3,
        out_specs=(vmem,) * 6,
        scratch_shapes=[
            wide, wide, wide, wide, V((toks, feat), BF),
            V((units, slots), BF), V((units, slots), BF), V((slots, slots), BF), V((units, width), BF),
            V((slots, width + 128), BF), V((n_exp * slots // n_seq, feat), BF),
            V((slots // n_seq, 128), F32), V((units, slots), F32), V((units, width), F32),
            V((units, slots), BF), V((8, slots), F32),
            V((n_seq, 8, 128), F32), V((n_seq, 8, 128), F32),
            V((8, 128), F32), V((n_exp, 8, 128), F32),
            V((n_seq, 144, 128), BF), V((n_seq, 144, 128), BF),
            V((n_seq, 128, 128), BF), V((n_seq, 128, 128), BF),
            V(log_decay.shape[::-1], F32),
            dma((7,)),
            dma((n_exp,)), dma((n_exp,)), dma((n_seq,)), dma((n_seq,)), dma((n_seq,)), dma((n_seq,)),
            dma((len(MSGS),)), dma((len(MSGS),)), dma((n_seq,)), dma((n_seq,)), dma((n_exp,)), dma((n_exp,)),
        ],
        compiler_params=pltpu.CompilerParams(
            collective_id=0, has_side_effects=True, vmem_limit_bytes=48 * 1024 * 1024
        ),
    )(
        queries, keys, values, attn_grad, moe_grad, hidden_acts[0].T, down_weight[0],
        log_decay.T, gate_probs.T, expert_ids.T,
    )
    out = pl.pallas_call(
        write_out,
        out_shape=tuple(jax.ShapeDtypeStruct(*s) for s in shapes),
        in_specs=[vmem] * 6,
        out_specs=(hbm,) * 6,
        scratch_shapes=[dma((6,))],
        compiler_params=pltpu.CompilerParams(vmem_limit_bytes=1024 * 1024),
    )(*held)
    return (*out[:3], out[3].T[None], out[4][None], out[5].T)


def solution(mesh):
    return jax.shard_map(
        on_device,
        mesh=mesh,
        in_specs=(
            P("seq", "exp"),
            P("seq", "exp"),
            P("seq", "exp"),
            P("seq", "exp"),
            P("seq", "exp"),
            P("seq", "exp"),
            P("seq", None),
            P("seq", None),
            P("exp", None, "seq"),
            P("exp", "seq", None),
        ),
        out_specs=(
            P("seq", "exp"),
            P("seq", "exp"),
            P("seq", "exp"),
            P("exp", None, "seq"),
            P("exp", "seq", None),
            P("seq", None),
        ),
        check_vma=False,
    )
```

```python
import functools

import jax
import jax.numpy as jnp
from jax import lax
from jax.experimental import pallas as pl
from jax.experimental.pallas import tpu as pltpu
from jax.sharding import PartitionSpec as P

MESH = pl.DeviceIdType.MESH
BF, F32, I32 = jnp.bfloat16, jnp.float32, jnp.int32
NX, NY = 4, 4

OFFS = [
    (0, 0), (-1, 0), (1, 0), (0, -1), (0, 1), (2, 0), (0, 2), (-1, -1),
    (1, -1), (-1, 1), (1, 1), (2, -1), (2, 1), (-1, 2), (1, 2), (2, 2),
]
SLOT = {off: i for i, off in enumerate(OFFS)}
DIRS = {"xp": (1, 0), "xm": (-1, 0), "yp": (0, 1), "ym": (0, -1)}
H1, H2, H1b, H1a, H2a, H2b = (0, 2), (2, 4), (0, 1), (1, 2), (2, 3), (3, 4)

NZ = 4
REL = [(0, 0), (0, 1), (1, 0), (1, 1), (-1, 0), (-1, 1), (2, 0), (2, 1)]
REL_SLOT = {r: i for i, r in enumerate(REL)}

START = [[(d, (0, 0), q) for d in ("xp", "xm", "yp", "ym")] for q in (H1b, H1a, H2a, H2b)]
ROUND1 = [
    [
        ([("xp", (0, 0), H1b)], []),
        ([("xm", (0, 0), H1b)], [("xm", (1, 0), H1b)]),
        ([("ym", (0, 0), H1b)], [("ym", (0, 1), H1b)]),
        ([("yp", (0, 0), H1b)], []),
    ],
    [
        ([("xp", (0, 0), H1a)], [("xp", (-1, 0), H1a), ("yp", (-1, 0), H1), ("ym", (-1, 0), H1)]),
        ([("xm", (0, 0), H1a)], [("yp", (1, 0), H1), ("ym", (1, 0), H1)]),
        ([("yp", (0, 0), H1a)], [("yp", (0, -1), H1a)]),
        ([("ym", (0, 0), H1a)], []),
    ],
    [
        ([("yp", (0, 0), H2a)], [("yp", (0, -1), H2a)]),
        ([("xp", (0, 0), H2a)], [("xp", (-1, 0), H2a)]),
        ([("ym", (0, 0), H2a)], []),
        ([("xm", (0, 0), H2a)], []),
    ],
    [
        ([("yp", (0, 0), H2b)], [("xp", (0, -1), H2), ("xm", (0, -1), H2)]),
        ([("ym", (0, 0), H2b)], [("ym", (0, 1), H2b), ("xp", (0, 1), H2), ("xm", (0, 1), H2)]),
        ([("xm", (0, 0), H2b)], [("xm", (1, 0), H2b)]),
        ([("xp", (0, 0), H2b)], []),
    ],
]
ROUND2 = [
    ([("xp", (-1, 0), H1a), ("xm", (1, 0), H1b)], [("yp", (2, 0), H1), ("ym", (2, 0), H1)]),
    ([("yp", (0, -1), H2a), ("ym", (0, 1), H2b)], [("xp", (0, 2), H2), ("xm", (0, 2), H2)]),
    ([("xp", (0, -1), H2)], [("xp", (-1, -1), H2a)]),
    ([("xm", (0, -1), H2)], [("xm", (1, -1), H2b)]),
    ([("yp", (-1, 0), H1)], [("yp", (-1, -1), H1a)]),
    ([("ym", (-1, 0), H1)], [("ym", (-1, 1), H1b)]),
    ([("xp", (0, 1), H2)], [("xp", (-1, 1), H2a)]),
    ([("xm", (0, 1), H2)], [("xm", (1, 1), H2b)]),
    ([("yp", (1, 0), H1)], [("yp", (1, -1), H1a)]),
    ([("ym", (1, 0), H1)], [("ym", (1, 1), H1b)]),
    ([("xp", (-1, 0), H2a), ("xm", (1, 0), H2b), ("yp", (0, -1), H1a), ("ym", (0, 1), H1b)], []),
]
ROUND3 = [
    ([("yp", (2, 0), H1)], [("yp", (2, -1), H1a)]),
    ([("ym", (2, 0), H1)], [("ym", (2, 1), H1b)]),
    ([("xp", (0, 2), H2)], [("xp", (-1, 2), H2a)]),
    ([("xm", (0, 2), H2)], [("xm", (1, 2), H2b)]),
]
ROUND4 = [
    ([("xp", (-1, -1), H2a), ("xp", (-1, 1), H2a), ("xm", (1, -1), H2b), ("xm", (1, 1), H2b)], []),
    ([("yp", (-1, -1), H1a), ("yp", (1, -1), H1a), ("ym", (-1, 1), H1b), ("ym", (1, 1), H1b)], []),
    ([("yp", (2, -1), H1a), ("ym", (2, 1), H1b), ("xp", (-1, 2), H2a), ("xm", (1, 2), H2b)], []),
]
MSGS = sum(START, []) + [m for r in (*ROUND1, ROUND2, ROUND3) for _, sends in r for m in sends]
INDEX = {m: i for i, m in enumerate(MSGS)}

FULL, A = (0, 4), (1, 3)
RAW_START = [(d, (0, 0), FULL) for d in ("xp", "xm", "yp", "ym")]
RAW1 = [
    ([("xp", (0, 0), FULL)], [("xp", (-1, 0), A), ("yp", (-1, 0), H1), ("ym", (-1, 0), H1)]),
    ([("xm", (0, 0), FULL)], [
        ("xm", (1, 0), H1b), ("xm", (1, 0), H2b), ("yp", (1, 0), H1), ("ym", (1, 0), H1)]),
    ([("yp", (0, 0), FULL)], [("yp", (0, -1), A), ("xp", (0, -1), H2), ("xm", (0, -1), H2)]),
    ([("ym", (0, 0), FULL)], [
        ("ym", (0, 1), H2b), ("ym", (0, 1), H1b), ("xp", (0, 1), H2), ("xm", (0, 1), H2)]),
]
RAW2 = [
    ([("xp", (-1, 0), A), ("xm", (1, 0), H1b)], ROUND2[0][1]),
    ([("yp", (0, -1), A), ("ym", (0, 1), H2b)], ROUND2[1][1]),
    *ROUND2[2:10],
    ([("xm", (1, 0), H2b), ("ym", (0, 1), H1b)], []),
]
RAW_MSGS = RAW_START + [m for r in (RAW1, RAW2, ROUND3) for _, sends in r for m in sends]
RAW_INDEX = {m: i for i, m in enumerate(RAW_MSGS)}
RAW = 256


def wrap(a, d):
    return tuple((p - q + 1) % 4 - 1 for p, q in zip(a, d))


def nn(a, b):
    return jnp.dot(a, b, preferred_element_type=F32)


def nt(a, b):
    return lax.dot_general(a, b, (((1,), (1,)), ((), ())), preferred_element_type=F32)


def iota(shape, axis):
    return lax.broadcasted_iota(I32, shape, axis)


def to_row(col, rows):
    eye = iota((rows, 128), 0) == iota((rows, 128), 1)
    return jnp.sum(jnp.where(eye, jnp.broadcast_to(col, (rows, 128)), 0.0), axis=0, keepdims=True)


def to_col(row):
    eye = iota((128, 128), 0) == iota((128, 128), 1)
    return jnp.sum(jnp.where(eye, jnp.broadcast_to(row, (128, 128)), 0.0), axis=1, keepdims=True)


def kernel(
    q_hbm, k_hbm, v_hbm, g_hbm, moe_hbm, hid_hbm, w_hbm, decay, gates, ids,
    qo, ko, vo, ho_out, wg, gate_out,
    qb, kb, vb, gb, moe, raw, raw_pack, hid, hid_t, order, w, x, pack, sel, back, acc, ho, parts,
    parts_s, parts_r, tok_s, tok_r, st_s, st_r, res_s, res_r, cum,
    load_sem, z_send, z_recv, a_send, a_recv, b_send, b_recv,
    x_send, x_recv, r_send, r_recv, y_send, y_recv, p_send, p_recv, t_send, t_recv,
):
    n_seq, n_exp = lax.axis_size("seq"), lax.axis_size("exp")
    me, e = lax.axis_index("seq"), lax.axis_index("exp")
    my_y, my_x = me // NX, me % NX
    cap = x.shape[0] // n_seq
    feat = moe.shape[1]
    width = w.shape[1]
    heads = decay.shape[0]
    toks = moe.shape[0]
    tall = toks + 16
    thin = feat - RAW
    gate_at = n_exp * thin
    raw_at = gate_at + 128
    quarter = gate_at // 4
    my_z, my_core = e // 2, e % 2

    def exp_at(rel):
        return ((my_z + rel[0] + NZ) % NZ) * 2 + (my_core + rel[1]) % 2

    def seq_at(off):
        return ((my_y + off[1] + NY) % NY) * NX + (my_x + off[0] + NX) % NX

    def remote(src, dst, ss, rs, where):
        return pltpu.make_async_remote_copy(
            src_ref=src, dst_ref=dst, send_sem=ss, recv_sem=rs,
            device_id=where, device_id_type=MESH,
        )

    loads = [
        (moe_hbm, moe), (q_hbm, qb), (k_hbm, kb), (v_hbm, vb), (g_hbm, gb), (hid_hbm, hid)
    ]
    loads.append((moe_hbm.at[:, pl.ds(thin, RAW)], raw.at[pl.ds(0, toks)]))
    for i, rel in enumerate(REL):
        first = pl.multiple_of(exp_at(rel) * feat, 128)
        loads.append((w_hbm.at[:, pl.ds(first, thin)], w.at[:, pl.ds(i * thin, thin)]))
        loads.append((w_hbm.at[:, pl.ds(first + thin, RAW)], w.at[:, pl.ds(gate_at + i * RAW, RAW)]))
    loads = [pltpu.make_async_copy(a, b, load_sem.at[i]) for i, (a, b) in enumerate(loads)]
    for c in loads:
        c.start()

    barrier = pltpu.get_barrier_semaphore()
    for off in range(1, n_seq):
        pl.semaphore_signal(barrier, inc=1, device_id={"seq": (me + off) % n_seq}, device_id_type=MESH)
    for off in range(1, n_exp):
        pl.semaphore_signal(barrier, inc=1, device_id={"exp": (e + off) % n_exp}, device_id_type=MESH)

    def span(q):
        stop = raw_at if q[1] == 4 else q[1] * quarter
        return pl.ds(q[0] * quarter, stop - q[0] * quarter)

    def message(m):
        d, off, q = m
        i = INDEX[m]
        src = x.at[pl.ds(SLOT[off] * cap, cap), span(q)]
        dst = x.at[pl.ds(SLOT[wrap(off, DIRS[d])] * cap, cap), span(q)]
        return remote(src, dst, x_send.at[i], x_recv.at[i], {"seq": seq_at(DIRS[d])})

    def go(steps):
        for waits, sends in steps:
            for m in waits:
                message(m).wait_recv()
            for m in sends:
                message(m).start()

    def raw_message(m):
        d, off, q = m
        i = RAW_INDEX[m]
        first = q[0] * toks // 4
        count = (tall if q[1] == 4 else q[1] * toks // 4) - first
        src = raw.at[pl.ds(SLOT[off] * tall + first, count)]
        dst = raw.at[pl.ds(SLOT[wrap(off, DIRS[d])] * tall + first, count)]
        return remote(src, dst, r_send.at[i], r_recv.at[i], {"seq": seq_at(DIRS[d])})

    def go_raw(steps):
        for waits, sends in steps:
            for m in waits:
                raw_message(m).wait_recv()
            for m in sends:
                raw_message(m).start()

    ids_f = ids[...].astype(F32)
    gates_f = gates[...].astype(F32)
    e_f = e.astype(F32)
    id_rows = [ids_f[k:k + 1, :] for k in range(2)]
    line = iota((16, 128), 0)
    id_tile = jnp.where(line == 0, id_rows[0], jnp.where(line == 1, id_rows[1], 0.0)).astype(BF)
    raw[toks:tall, :] = jnp.concatenate([id_tile] * (RAW // 128), axis=1)
    loads[6].wait()
    pl.semaphore_wait(barrier, n_seq - 1 + n_exp - 1)
    go_raw([([], RAW_START)])

    expert = iota((n_exp, 128), 0).astype(F32)
    routed = jnp.where((expert == id_rows[0]) | (expert == id_rows[1]), 1.0, 0.0)
    upto = jnp.where(iota((128, 128), 0) <= iota((128, 128), 1), 1.0, 0.0).astype(BF)
    rank = nn(routed.astype(BF), upto) - 1.0
    rank = jnp.where(routed > 0.0, rank, -1.0)
    slot_no = iota((cap, 128), 0).astype(F32)
    loads[0].wait()
    for i in range(n_exp):
        chosen = jnp.where(rank[i:i + 1, :] == slot_no, 1.0, 0.0)
        pack[pl.ds(i * cap, cap), :] = nn(chosen.astype(BF), moe[:, 0:thin]).astype(BF)
    own_rank = jnp.max(jnp.where(expert == e_f, rank, -1.0), axis=0, keepdims=True)
    own = jnp.where(own_rank == slot_no, 1.0, 0.0)
    sel[...] = own
    tok_gate = sum(jnp.where(id_rows[k] == e_f, gates_f[k:k + 1, :], 0.0) for k in range(2))
    slot_gate = jnp.sum(own * tok_gate, axis=1, keepdims=True)
    x[0:cap, gate_at:raw_at] = jnp.broadcast_to(slot_gate, (cap, 128)).astype(BF)

    z_copies = []
    for i, rel in enumerate(REL):
        if i > 0:
            peer = exp_at(rel)
            there = REL_SLOT[((-rel[0] + 1) % NZ - 1, rel[1])]
            z_copies.append(remote(
                pack.at[pl.ds(pl.multiple_of(peer * cap, 16), cap)],
                x.at[pl.ds(0, cap), pl.ds(there * thin, thin)],
                z_send.at[there], z_recv.at[there], {"exp": peer}))
            z_copies[-1].start()
    z_recvs = [
        remote(pack.at[pl.ds(0, cap)], x.at[pl.ds(0, cap), pl.ds(i * thin, thin)],
               z_send.at[i], z_recv.at[i], {"exp": exp_at(REL[i])}) for i in range(1, n_exp)]
    x[0:cap, 0:thin] = pack[pl.ds(pl.multiple_of(e * cap, 16), cap), :]

    def begin(i):
        for c in z_recvs[max(2 * i - 1, 0):2 * i + 1]:
            c.wait_recv()
        go([([], START[i])])

    go_raw(RAW1)
    begin(0)

    cum[...] = jnp.dot(
        decay[...], jnp.where(iota((128, 128), 0) <= iota((128, 128), 1), 1.0, 0.0),
        preferred_element_type=F32, precision=lax.Precision.HIGHEST)
    for c in loads[1:5]:
        c.wait()

    def head_terms(h):
        row = jnp.sum(jnp.where(iota((heads, 128), 0) == h, cum[...], 0.0), axis=0, keepdims=True)
        col = to_col(row)
        return row, col, col[127:128, :]

    def local_state(h, carry):
        row, col, total = head_terms(h)
        cols = pl.ds(pl.multiple_of(h * 128, 128), 128)
        kw = (kb[:, cols].astype(F32) * jnp.exp(total - col)).T.astype(BF)
        qw = (qb[:, cols].astype(F32) * jnp.exp(col)).T.astype(BF)
        kv = nn(kw, vb[:, cols]).astype(BF)
        qg = nn(qw, gb[:, cols]).astype(BF)
        gain = jnp.broadcast_to(jnp.exp(total), (16, 128))
        hi = gain.astype(BF).astype(F32)
        mid = (gain - hi).astype(BF).astype(F32)
        low = gain - hi - mid
        three = jnp.where(line == 0, hi, jnp.where(line == 1, mid, jnp.where(line == 2, low, 0.0))).astype(BF)
        for p in range(2):
            st_s[2 * h + p, 0:64, :] = kv[64 * p:64 * p + 64, :]
            st_s[2 * h + p, 64:128, :] = qg[64 * p:64 * p + 64, :]
            st_s[2 * h + p, 128:144, :] = three
        return carry

    lax.fori_loop(0, heads, local_state, 0)
    go_raw(RAW2)
    begin(1)
    go_raw(ROUND3)
    a_copies = []
    for off in range(1, n_seq):
        peer = (me + off) % n_seq
        a_copies.append(remote(st_s.at[peer], st_r.at[me], a_send.at[off], a_recv.at[off], {"seq": peer}))
        a_copies[-1].start()
    st_r[me] = st_s[me]
    begin(2)
    begin(3)

    n_rows = x.shape[0]
    place = iota((1, n_rows), 1)
    source = place
    for i, off in enumerate(OFFS):
        inside = (place >= i * cap) & (place < (i + 1) * cap)
        source = source + jnp.where(inside, (seq_at(off) - i) * cap, 0)

    def make_order(i, carry):
        first = pl.multiple_of(i * 64, 64)
        hit = iota((64, n_rows), 0) + first == source
        order[pl.ds(first, 64), :] = jnp.where(hit, 1.0, 0.0).astype(BF)
        return carry

    lax.fori_loop(0, n_rows // 64, make_order, 0)
    loads[5].wait()
    hid_t[...] = nn(hid[...], order[...]).astype(BF)

    go_raw(ROUND4)

    def pack_block(i, carry):
        tile = raw[pl.ds(pl.multiple_of(i * tall + toks, 16), 16), 0:128].astype(F32)
        id0, id1 = tile[0:1, :], tile[1:2, :]
        routed = jnp.where((expert == id0) | (expert == id1), 1.0, 0.0)
        rank = jnp.where(routed > 0.0, nn(routed.astype(BF), upto) - 1.0, -1.0)
        chosen = jnp.concatenate(
            [jnp.where(rank[j:j + 1, :] == slot_no, 1.0, 0.0).astype(BF) for j in range(n_exp)], axis=0)
        rows = nn(chosen, raw[pl.ds(pl.multiple_of(i * tall, 16), toks), :]).astype(BF)
        for j in range(n_exp):
            raw_pack[j, pl.ds(pl.multiple_of(i * cap, 16), cap), :] = rows[j * cap:(j + 1) * cap, :]
        return carry

    lax.fori_loop(0, n_seq, pack_block, 0)
    cut = 512
    y_copies, y_recvs = [], []
    for part, (first, count) in enumerate([(0, cut), (cut, n_rows - cut)]):
        rows = pl.ds(first, count)
        y_recvs.append([])
        for i, rel in enumerate(REL[1:], 1):
            peer = exp_at(rel)
            there = REL_SLOT[((-rel[0] + 1) % NZ - 1, rel[1])]
            c = remote(
                raw_pack.at[peer, rows], x.at[rows, pl.ds(raw_at + there * RAW, RAW)],
                y_send.at[part, there], y_recv.at[part, there], {"exp": peer})
            c.start()
            y_copies.append(c)
            y_recvs[-1].append(remote(
                raw_pack.at[peer, rows], x.at[rows, pl.ds(raw_at + i * RAW, RAW)],
                y_send.at[part, i], y_recv.at[part, i], {"exp": peer}))
    x[:, raw_at:raw_at + RAW] = raw_pack[e]

    go(ROUND1[0])

    for c in a_copies:
        c.wait_recv()

    def gain_of(b):
        g3 = st_r[b, 128:144, :].astype(F32)
        return g3[0:1, :] + g3[1:2, :] + g3[2:3, :]

    def scan_up(b, state):
        res_s[b, 0:64, :] = state.astype(BF)
        return gain_of(b) * state + st_r[b, 0:64, :].astype(F32)

    def scan_down(i, state):
        b = n_seq - 1 - i
        res_s[b, 64:128, :] = state.astype(BF)
        return gain_of(b) * state + st_r[b, 64:128, :].astype(F32)

    zero = jnp.zeros((64, 128), F32)
    lax.fori_loop(0, n_seq, scan_up, zero)
    lax.fori_loop(0, n_seq, scan_down, zero)
    b_copies = []
    for off in range(1, n_seq):
        peer = (me + off) % n_seq
        b_copies.append(remote(res_s.at[peer], res_r.at[me], b_send.at[off], b_recv.at[off], {"seq": peer}))
        b_copies[-1].start()
    res_r[me] = res_s[me]

    for step in ROUND1[1:]:
        go(step)

    for c in b_copies:
        c.wait_recv()

    def finish_head(h, carry):
        row, col, total = head_terms(h)
        cols = pl.ds(pl.multiple_of(h * 128, 128), 128)
        q, k, v, g = qb[:, cols], kb[:, cols], vb[:, cols], gb[:, cols]
        two = res_r[pl.ds(2 * h, 2)]
        inc = two[:, 0:64, :].reshape(128, 128)
        upc = two[:, 64:128, :].reshape(128, 128)
        lead, tail = jnp.exp(col), jnp.exp(total - col)
        spread = jnp.broadcast_to(col, (128, 128)) - jnp.broadcast_to(row, (128, 128))
        causal = iota((128, 128), 0) >= iota((128, 128), 1)
        mask = jnp.exp(jnp.where(causal, spread, -jnp.inf))
        gs = nt(g, v) * mask
        qk = nt(q, k) * mask
        qo[:, cols] = (nn(gs.astype(BF), k) + lead * nt(g, inc)).astype(BF)
        ko[:, cols] = (nn(gs.T.astype(BF), q) + tail * nt(v, upc)).astype(BF)
        vo[:, cols] = (nn(qk.T.astype(BF), g) + tail * nn(k, upc)).astype(BF)
        return carry

    lax.fori_loop(0, heads, finish_head, 0)

    chunk = 512
    chunks = width // chunk
    units = w.shape[0]

    def x_cols(i):
        return pl.ds(pl.multiple_of(i * chunk + jnp.where(i * chunk >= gate_at, 128, 0), 128), chunk)

    wide = gate_at // chunk

    def product(start, count, lo, hi):
        rows = pl.ds(start, count)
        if lo == 0:
            back[:, rows] = jnp.zeros((units, count), F32)

        def one(i, carry):
            cols = pl.ds(pl.multiple_of(i * chunk, chunk), chunk)
            back[:, rows] += nt(w[:, cols], x[rows, x_cols(i)])
            return carry

        lax.fori_loop(lo, hi, one, 0)

    def use_product(start, count):
        rows = pl.ds(start, count)
        first = jnp.where(iota((8, 128), 1) == 0, 1.0, 0.0).astype(BF)
        gate = nt(first, x[rows, gate_at:raw_at])[0:1, :]

        def after(i, total):
            part = pl.ds(pl.multiple_of(i * 64, 64), 64)
            b = back[part, rows]
            ho[part, rows] = (gate * b).astype(BF)
            return total + jnp.sum(b * hid_t[part, rows].astype(F32), axis=0, keepdims=True)

        total = lax.fori_loop(0, units // 64, after, jnp.zeros((1, count), F32))
        parts[0:1, rows] = total

    def scaled(start, count, cols):
        rows = pl.ds(start, count)
        gate = x[rows, gate_at:raw_at]
        return x[rows, cols] * jnp.concatenate([gate] * (chunk // 128), axis=1)

    p_copies = []
    parts_s[...] = jnp.zeros_like(parts_s)

    def hand_out(first, last):
        for i in range(first, last):
            parts_s[i, 0:1, 0:cap] = parts[0:1, i * cap:(i + 1) * cap]
            if i > 0:
                owner = {"seq": seq_at(OFFS[i])}
                c = remote(parts_s.at[i], parts_r.at[i], p_send.at[i], p_recv.at[i], owner)
                c.start()
                p_copies.append(c)

    def first_grad(i, carry):
        cols = pl.ds(pl.multiple_of(i * chunk, chunk), chunk)
        acc[:, cols] = nn(hid_t[:, 0:cut], scaled(0, cut, x_cols(i)))
        return carry

    for c in loads[7:]:
        c.wait()
    go(ROUND2[:6] + ROUND2[-1:])
    product(0, cut // 2, 0, wide)
    go(ROUND2[6:10])
    product(cut // 2, cut // 2, 0, wide)
    go(ROUND3)
    lax.fori_loop(0, wide, first_grad, 0)
    for c in y_recvs[0]:
        c.wait_recv()
    product(0, cut, wide, chunks)
    use_product(0, cut)
    hand_out(0, cut // cap)
    lax.fori_loop(wide, chunks, first_grad, 0)
    go(ROUND4)
    for c in y_recvs[1]:
        c.wait_recv()
    product(cut, n_rows - cut, 0, chunks)
    use_product(cut, n_rows - cut)
    hand_out(cut // cap, n_seq)

    def last_grad(i, carry):
        cols = pl.ds(pl.multiple_of(i * chunk, chunk), chunk)
        wg[:, cols] = (acc[:, cols] + nn(hid_t[:, cut:], scaled(cut, n_rows - cut, x_cols(i)))).astype(BF)
        return carry

    lax.fori_loop(0, chunks, last_grad, 0)
    ho_out[...] = nt(ho[...], order[...]).astype(BF)

    total = parts_s[0]
    for i, c in enumerate(p_copies):
        c.wait_recv()
        total = total + parts_r[i + 1]
    per_tok = jnp.sum(sel[...] * to_col(total[0:1, :])[0:cap, :], axis=0, keepdims=True)
    tok_s[...] = jnp.broadcast_to(per_tok, (8, 128))
    t_copies = []
    for off in range(1, n_exp):
        peer = (e + off) % n_exp
        t_copies.append(remote(tok_s, tok_r.at[e], t_send.at[off], t_recv.at[off], {"exp": peer}))
        t_copies[-1].start()
    tok_r[e] = tok_s[...]
    for c in t_copies:
        c.wait_recv()
    for k in range(2):
        gate_out[k:k + 1, :] = sum(
            jnp.where(id_rows[k] == float(i), tok_r[i, 0:1, :], 0.0) for i in range(n_exp))

    for c in z_copies + y_copies + a_copies + b_copies + p_copies + t_copies:
        c.wait_send()
    for m in MSGS:
        message(m).wait_send()
    for m in RAW_MSGS:
        raw_message(m).wait_send()


def write_out(q_in, k_in, v_in, ho_in, wg_in, gate_in, q_out, k_out, v_out, ho_out, wg_out, gate_out, sem):
    e = lax.axis_index("exp")
    feat = wg_in.shape[1] // len(REL)
    thin = feat - RAW
    pairs = []
    for i, (z, core) in enumerate(REL):
        there = ((e // 2 + z + NZ) % NZ) * 2 + (e % 2 + core) % 2
        first = pl.multiple_of(there * feat, 128)
        pairs.append((wg_in.at[:, pl.ds(i * thin, thin)], wg_out.at[:, pl.ds(first, thin)]))
        raw_in = wg_in.at[:, pl.ds(len(REL) * thin + i * RAW, RAW)]
        pairs.append((raw_in, wg_out.at[:, pl.ds(first + thin, RAW)]))
    pairs += [(q_in, q_out), (k_in, k_out), (v_in, v_out), (ho_in, ho_out), (gate_in, gate_out)]
    copies = [pltpu.make_async_copy(a, b, sem.at[i]) for i, (a, b) in enumerate(pairs)]
    for c in copies:
        c.start()
    for c in copies:
        c.wait()


def on_device(
    queries, keys, values, attn_grad, log_decay, moe_grad, gate_probs, expert_ids, hidden_acts, down_weight
):
    n_seq, n_exp = lax.axis_size("seq"), lax.axis_size("exp")
    _, slots, units = hidden_acts.shape
    width = down_weight.shape[2]
    toks, flat = queries.shape
    feat = moe_grad.shape[1]
    hbm = pl.BlockSpec(memory_space=pl.ANY)
    vmem = pl.BlockSpec(memory_space=pltpu.VMEM)
    dma = pltpu.SemaphoreType.DMA
    V = pltpu.VMEM
    wide = V((toks, flat), BF)
    shapes = [
        ((toks, flat), BF), ((toks, flat), BF), ((toks, flat), BF),
        ((units, slots), BF), ((units, width), BF), ((2, toks), F32),
    ]
    held = pl.pallas_call(
        kernel,
        out_shape=tuple(V(*s) for s in shapes),
        in_specs=[hbm] * 7 + [vmem] * 3,
        out_specs=(vmem,) * 6,
        scratch_shapes=[
            wide, wide, wide, wide, V((toks, feat), BF),
            V((n_seq * (toks + 16), RAW), BF), V((n_exp, slots, RAW), BF), V((units, slots), BF), V((units, slots), BF), V((slots, slots), BF), V((units, width), BF),
            V((slots, width + 128), BF), V((n_exp * slots // n_seq, feat - RAW), BF),
            V((slots // n_seq, 128), F32), V((units, slots), F32), V((units, width), F32),
            V((units, slots), BF), V((8, slots), F32),
            V((n_seq, 8, 128), F32), V((n_seq, 8, 128), F32),
            V((8, 128), F32), V((n_exp, 8, 128), F32),
            V((n_seq, 144, 128), BF), V((n_seq, 144, 128), BF),
            V((n_seq, 128, 128), BF), V((n_seq, 128, 128), BF),
            V(log_decay.shape[::-1], F32),
            dma((7 + 2 * n_exp,)),
            dma((n_exp,)), dma((n_exp,)), dma((n_seq,)), dma((n_seq,)), dma((n_seq,)), dma((n_seq,)),
            dma((len(MSGS),)), dma((len(MSGS),)), dma((len(RAW_MSGS),)), dma((len(RAW_MSGS),)),
            dma((2, n_exp)), dma((2, n_exp)), dma((n_seq,)), dma((n_seq,)), dma((n_exp,)), dma((n_exp,)),
        ],
        compiler_params=pltpu.CompilerParams(
            collective_id=0, has_side_effects=True, vmem_limit_bytes=53 * 1024 * 1024
        ),
    )(
        queries, keys, values, attn_grad, moe_grad, hidden_acts[0].T, down_weight[0],
        log_decay.T, gate_probs.T, expert_ids.T,
    )
    out = pl.pallas_call(
        write_out,
        out_shape=tuple(jax.ShapeDtypeStruct(*s) for s in shapes),
        in_specs=[vmem] * 6,
        out_specs=(hbm,) * 6,
        scratch_shapes=[dma((5 + 2 * n_exp,))],
        compiler_params=pltpu.CompilerParams(vmem_limit_bytes=1024 * 1024),
    )(*held)
    return (*out[:3], out[3].T[None], out[4][None], out[5].T)


def solution(mesh):
    return jax.shard_map(
        on_device,
        mesh=mesh,
        in_specs=(
            P("seq", "exp"),
            P("seq", "exp"),
            P("seq", "exp"),
            P("seq", "exp"),
            P("seq", "exp"),
            P("seq", "exp"),
            P("seq", None),
            P("seq", None),
            P("exp", None, "seq"),
            P("exp", "seq", None),
        ),
        out_specs=(
            P("seq", "exp"),
            P("seq", "exp"),
            P("seq", "exp"),
            P("exp", None, "seq"),
            P("exp", "seq", None),
            P("seq", None),
        ),
        check_vma=False,
    )
```

```python
import functools

import jax
import jax.numpy as jnp
from jax import lax
from jax.experimental import pallas as pl
from jax.experimental.pallas import tpu as pltpu
from jax.sharding import PartitionSpec as P

MESH = pl.DeviceIdType.MESH
BF, F32, I32 = jnp.bfloat16, jnp.float32, jnp.int32
NX, NY = 4, 4

OFFS = [
    (0, 0), (-1, 0), (1, 0), (0, -1), (0, 1), (2, 0), (0, 2), (-1, -1),
    (1, -1), (-1, 1), (1, 1), (2, -1), (2, 1), (-1, 2), (1, 2), (2, 2),
]
SLOT = {off: i for i, off in enumerate(OFFS)}
DIRS = {"xp": (1, 0), "xm": (-1, 0), "yp": (0, 1), "ym": (0, -1)}
H1, H2, H1b, H1a, H2a, H2b = (0, 2), (2, 4), (0, 1), (1, 2), (2, 3), (3, 4)

NZ = 4
REL = [(0, 0), (0, 1), (1, 0), (1, 1), (-1, 0), (-1, 1), (2, 0), (2, 1)]
REL_SLOT = {r: i for i, r in enumerate(REL)}

START = [[(d, (0, 0), q) for d in ("xp", "xm", "yp", "ym")] for q in (H1b, H1a, H2a, H2b)]
ROUND1 = [
    [
        ([("xp", (0, 0), H1b)], []),
        ([("xm", (0, 0), H1b)], [("xm", (1, 0), H1b)]),
        ([("ym", (0, 0), H1b)], [("ym", (0, 1), H1b)]),
        ([("yp", (0, 0), H1b)], []),
    ],
    [
        ([("xp", (0, 0), H1a)], [("xp", (-1, 0), H1a), ("yp", (-1, 0), H1), ("ym", (-1, 0), H1)]),
        ([("xm", (0, 0), H1a)], [("yp", (1, 0), H1), ("ym", (1, 0), H1)]),
        ([("yp", (0, 0), H1a)], [("yp", (0, -1), H1a)]),
        ([("ym", (0, 0), H1a)], []),
    ],
    [
        ([("yp", (0, 0), H2a)], [("yp", (0, -1), H2a)]),
        ([("xp", (0, 0), H2a)], [("xp", (-1, 0), H2a)]),
        ([("ym", (0, 0), H2a)], []),
        ([("xm", (0, 0), H2a)], []),
    ],
    [
        ([("yp", (0, 0), H2b)], [("xp", (0, -1), H2), ("xm", (0, -1), H2)]),
        ([("ym", (0, 0), H2b)], [("ym", (0, 1), H2b), ("xp", (0, 1), H2), ("xm", (0, 1), H2)]),
        ([("xm", (0, 0), H2b)], [("xm", (1, 0), H2b)]),
        ([("xp", (0, 0), H2b)], []),
    ],
]
ROUND2 = [
    ([("xp", (-1, 0), H1a), ("xm", (1, 0), H1b)], [("yp", (2, 0), H1), ("ym", (2, 0), H1)]),
    ([("yp", (0, -1), H2a), ("ym", (0, 1), H2b)], [("xp", (0, 2), H2), ("xm", (0, 2), H2)]),
    ([("xp", (0, -1), H2)], [("xp", (-1, -1), H2a)]),
    ([("xm", (0, -1), H2)], [("xm", (1, -1), H2b)]),
    ([("yp", (-1, 0), H1)], [("yp", (-1, -1), H1a)]),
    ([("ym", (-1, 0), H1)], [("ym", (-1, 1), H1b)]),
    ([("xp", (0, 1), H2)], [("xp", (-1, 1), H2a)]),
    ([("xm", (0, 1), H2)], [("xm", (1, 1), H2b)]),
    ([("yp", (1, 0), H1)], [("yp", (1, -1), H1a)]),
    ([("ym", (1, 0), H1)], [("ym", (1, 1), H1b)]),
    ([("xp", (-1, 0), H2a), ("xm", (1, 0), H2b), ("yp", (0, -1), H1a), ("ym", (0, 1), H1b)], []),
]
ROUND3 = [
    ([("yp", (2, 0), H1)], [("yp", (2, -1), H1a)]),
    ([("ym", (2, 0), H1)], [("ym", (2, 1), H1b)]),
    ([("xp", (0, 2), H2)], [("xp", (-1, 2), H2a)]),
    ([("xm", (0, 2), H2)], [("xm", (1, 2), H2b)]),
]
ROUND4 = [
    ([("xp", (-1, -1), H2a), ("xp", (-1, 1), H2a), ("xm", (1, -1), H2b), ("xm", (1, 1), H2b)], []),
    ([("yp", (-1, -1), H1a), ("yp", (1, -1), H1a), ("ym", (-1, 1), H1b), ("ym", (1, 1), H1b)], []),
    ([("yp", (2, -1), H1a), ("ym", (2, 1), H1b), ("xp", (-1, 2), H2a), ("xm", (1, 2), H2b)], []),
]
MSGS = sum(START, []) + [m for r in (*ROUND1, ROUND2, ROUND3) for _, sends in r for m in sends]
INDEX = {m: i for i, m in enumerate(MSGS)}

FULL, A = (0, 4), (1, 3)
RAW_START = [(d, (0, 0), FULL) for d in ("xp", "xm", "yp", "ym")]
RAW1 = [
    ([("xp", (0, 0), FULL)], [("xp", (-1, 0), A), ("yp", (-1, 0), H1), ("ym", (-1, 0), H1)]),
    ([("xm", (0, 0), FULL)], [
        ("xm", (1, 0), H1b), ("xm", (1, 0), H2b), ("yp", (1, 0), H1), ("ym", (1, 0), H1)]),
    ([("yp", (0, 0), FULL)], [("yp", (0, -1), A), ("xp", (0, -1), H2), ("xm", (0, -1), H2)]),
    ([("ym", (0, 0), FULL)], [
        ("ym", (0, 1), H2b), ("ym", (0, 1), H1b), ("xp", (0, 1), H2), ("xm", (0, 1), H2)]),
]
RAW2 = [
    ([("xp", (-1, 0), A), ("xm", (1, 0), H1b)], ROUND2[0][1]),
    ([("yp", (0, -1), A), ("ym", (0, 1), H2b)], ROUND2[1][1]),
    *ROUND2[2:10],
    ([("xm", (1, 0), H2b), ("ym", (0, 1), H1b)], []),
]
RAW_MSGS = RAW_START + [m for r in (RAW1, RAW2, ROUND3) for _, sends in r for m in sends]
RAW_INDEX = {m: i for i, m in enumerate(RAW_MSGS)}
RAW = 256


def wrap(a, d):
    return tuple((p - q + 1) % 4 - 1 for p, q in zip(a, d))


def nn(a, b):
    return jnp.dot(a, b, preferred_element_type=F32)


def nt(a, b):
    return lax.dot_general(a, b, (((1,), (1,)), ((), ())), preferred_element_type=F32)


def iota(shape, axis):
    return lax.broadcasted_iota(I32, shape, axis)


def to_row(col, rows):
    eye = iota((rows, 128), 0) == iota((rows, 128), 1)
    return jnp.sum(jnp.where(eye, jnp.broadcast_to(col, (rows, 128)), 0.0), axis=0, keepdims=True)


def to_col(row):
    eye = iota((128, 128), 0) == iota((128, 128), 1)
    return jnp.sum(jnp.where(eye, jnp.broadcast_to(row, (128, 128)), 0.0), axis=1, keepdims=True)


def kernel(
    q_hbm, k_hbm, v_hbm, g_hbm, moe_hbm, hid_hbm, w_hbm, decay, gates, ids,
    qo, ko, vo, ho_out, wg, gate_out,
    qb, kb, vb, gb, moe, raw, raw_pack, hid, hid_t, order, w, x, pack, sel, back, acc, ho, parts,
    parts_s, parts_r, tok_s, tok_r, st_s, st_r, res_s, res_r, cum,
    load_sem, z_send, z_recv, a_send, a_recv, b_send, b_recv,
    x_send, x_recv, r_send, r_recv, y_send, y_recv, p_send, p_recv, t_send, t_recv,
):
    n_seq, n_exp = lax.axis_size("seq"), lax.axis_size("exp")
    me, e = lax.axis_index("seq"), lax.axis_index("exp")
    my_y, my_x = me // NX, me % NX
    cap = x.shape[0] // n_seq
    feat = moe.shape[1]
    width = w.shape[1]
    heads = decay.shape[0]
    toks = moe.shape[0]
    tall = toks + 16
    thin = feat - RAW
    gate_at = n_exp * thin
    raw_at = gate_at + 128
    quarter = gate_at // 4
    my_z, my_core = e // 2, e % 2

    def exp_at(rel):
        return ((my_z + rel[0] + NZ) % NZ) * 2 + (my_core + rel[1]) % 2

    def seq_at(off):
        return ((my_y + off[1] + NY) % NY) * NX + (my_x + off[0] + NX) % NX

    def remote(src, dst, ss, rs, where):
        return pltpu.make_async_remote_copy(
            src_ref=src, dst_ref=dst, send_sem=ss, recv_sem=rs,
            device_id=where, device_id_type=MESH,
        )

    loads = [
        (moe_hbm, moe), (q_hbm, qb), (k_hbm, kb), (v_hbm, vb), (g_hbm, gb), (hid_hbm, hid)
    ]
    loads.append((moe_hbm.at[:, pl.ds(thin, RAW)], raw.at[pl.ds(0, toks)]))
    for i, rel in enumerate(REL):
        first = pl.multiple_of(exp_at(rel) * feat, 128)
        loads.append((w_hbm.at[:, pl.ds(first, thin)], w.at[:, pl.ds(i * thin, thin)]))
        loads.append((w_hbm.at[:, pl.ds(first + thin, RAW)], w.at[:, pl.ds(gate_at + i * RAW, RAW)]))
    loads = [pltpu.make_async_copy(a, b, load_sem.at[i]) for i, (a, b) in enumerate(loads)]
    for c in [loads[6]] + loads[:6]:
        c.start()

    barrier = pltpu.get_barrier_semaphore()
    for off in range(1, n_seq):
        pl.semaphore_signal(barrier, inc=1, device_id={"seq": (me + off) % n_seq}, device_id_type=MESH)
    for off in range(1, n_exp):
        pl.semaphore_signal(barrier, inc=1, device_id={"exp": (e + off) % n_exp}, device_id_type=MESH)

    def span(q):
        stop = raw_at if q[1] == 4 else q[1] * quarter
        return pl.ds(q[0] * quarter, stop - q[0] * quarter)

    def message(m):
        d, off, q = m
        i = INDEX[m]
        src = x.at[pl.ds(SLOT[off] * cap, cap), span(q)]
        dst = x.at[pl.ds(SLOT[wrap(off, DIRS[d])] * cap, cap), span(q)]
        return remote(src, dst, x_send.at[i], x_recv.at[i], {"seq": seq_at(DIRS[d])})

    def go(steps):
        for waits, sends in steps:
            for m in waits:
                message(m).wait_recv()
            for m in sends:
                message(m).start()

    def raw_message(m):
        d, off, q = m
        i = RAW_INDEX[m]
        first = q[0] * toks // 4
        count = (tall if q[1] == 4 else q[1] * toks // 4) - first
        src = raw.at[pl.ds(SLOT[off] * tall + first, count)]
        dst = raw.at[pl.ds(SLOT[wrap(off, DIRS[d])] * tall + first, count)]
        return remote(src, dst, r_send.at[i], r_recv.at[i], {"seq": seq_at(DIRS[d])})

    def go_raw(steps):
        for waits, sends in steps:
            for m in waits:
                raw_message(m).wait_recv()
            for m in sends:
                raw_message(m).start()

    ids_f = ids[...].astype(F32)
    gates_f = gates[...].astype(F32)
    e_f = e.astype(F32)
    id_rows = [ids_f[k:k + 1, :] for k in range(2)]
    line = iota((16, 128), 0)
    id_tile = jnp.where(line == 0, id_rows[0], jnp.where(line == 1, id_rows[1], 0.0)).astype(BF)
    raw[toks:tall, :] = jnp.concatenate([id_tile] * (RAW // 128), axis=1)
    loads[6].wait()
    pl.semaphore_wait(barrier, n_seq - 1 + n_exp - 1)
    go_raw([([], RAW_START)])

    expert = iota((n_exp, 128), 0).astype(F32)
    routed = jnp.where((expert == id_rows[0]) | (expert == id_rows[1]), 1.0, 0.0)
    upto = jnp.where(iota((128, 128), 0) <= iota((128, 128), 1), 1.0, 0.0).astype(BF)
    rank = nn(routed.astype(BF), upto) - 1.0
    rank = jnp.where(routed > 0.0, rank, -1.0)
    slot_no = iota((cap, 128), 0).astype(F32)
    loads[0].wait()
    for i in range(n_exp):
        chosen = jnp.where(rank[i:i + 1, :] == slot_no, 1.0, 0.0)
        pack[pl.ds(i * cap, cap), :] = nn(chosen.astype(BF), moe[:, 0:thin]).astype(BF)
    own_rank = jnp.max(jnp.where(expert == e_f, rank, -1.0), axis=0, keepdims=True)
    own = jnp.where(own_rank == slot_no, 1.0, 0.0)
    sel[...] = own
    tok_gate = sum(jnp.where(id_rows[k] == e_f, gates_f[k:k + 1, :], 0.0) for k in range(2))
    slot_gate = jnp.sum(own * tok_gate, axis=1, keepdims=True)
    x[0:cap, gate_at:raw_at] = jnp.broadcast_to(slot_gate, (cap, 128)).astype(BF)

    z_copies = []
    for i, rel in enumerate(REL):
        if i > 0:
            peer = exp_at(rel)
            there = REL_SLOT[((-rel[0] + 1) % NZ - 1, rel[1])]
            z_copies.append(remote(
                pack.at[pl.ds(pl.multiple_of(peer * cap, 16), cap)],
                x.at[pl.ds(0, cap), pl.ds(there * thin, thin)],
                z_send.at[there], z_recv.at[there], {"exp": peer}))
            z_copies[-1].start()
    for c in loads[7:]:
        c.start()
    z_recvs = [
        remote(pack.at[pl.ds(0, cap)], x.at[pl.ds(0, cap), pl.ds(i * thin, thin)],
               z_send.at[i], z_recv.at[i], {"exp": exp_at(REL[i])}) for i in range(1, n_exp)]
    x[0:cap, 0:thin] = pack[pl.ds(pl.multiple_of(e * cap, 16), cap), :]

    def begin(i):
        for c in z_recvs[max(2 * i - 1, 0):2 * i + 1]:
            c.wait_recv()
        go([([], START[i])])

    go_raw(RAW1)
    begin(0)

    cum[...] = jnp.dot(
        decay[...], jnp.where(iota((128, 128), 0) <= iota((128, 128), 1), 1.0, 0.0),
        preferred_element_type=F32, precision=lax.Precision.HIGHEST)
    for c in loads[1:5]:
        c.wait()

    def head_terms(h):
        row = jnp.sum(jnp.where(iota((heads, 128), 0) == h, cum[...], 0.0), axis=0, keepdims=True)
        col = to_col(row)
        return row, col, col[127:128, :]

    def local_state(h, carry):
        row, col, total = head_terms(h)
        cols = pl.ds(pl.multiple_of(h * 128, 128), 128)
        kw = (kb[:, cols].astype(F32) * jnp.exp(total - col)).T.astype(BF)
        qw = (qb[:, cols].astype(F32) * jnp.exp(col)).T.astype(BF)
        kv = nn(kw, vb[:, cols]).astype(BF)
        qg = nn(qw, gb[:, cols]).astype(BF)
        gain = jnp.broadcast_to(jnp.exp(total), (16, 128))
        hi = gain.astype(BF).astype(F32)
        mid = (gain - hi).astype(BF).astype(F32)
        low = gain - hi - mid
        three = jnp.where(line == 0, hi, jnp.where(line == 1, mid, jnp.where(line == 2, low, 0.0))).astype(BF)
        for p in range(2):
            st_s[2 * h + p, 0:64, :] = kv[64 * p:64 * p + 64, :]
            st_s[2 * h + p, 64:128, :] = qg[64 * p:64 * p + 64, :]
            st_s[2 * h + p, 128:144, :] = three
        return carry

    lax.fori_loop(0, heads, local_state, 0)
    go_raw(RAW2)
    begin(1)
    go_raw(ROUND3)
    a_copies = []
    for off in range(1, n_seq):
        peer = (me + off) % n_seq
        a_copies.append(remote(st_s.at[peer], st_r.at[me], a_send.at[off], a_recv.at[off], {"seq": peer}))
        a_copies[-1].start()
    st_r[me] = st_s[me]
    begin(2)
    begin(3)

    n_rows = x.shape[0]
    place = iota((1, n_rows), 1)
    source = place
    for i, off in enumerate(OFFS):
        inside = (place >= i * cap) & (place < (i + 1) * cap)
        source = source + jnp.where(inside, (seq_at(off) - i) * cap, 0)

    def make_order(i, carry):
        first = pl.multiple_of(i * 64, 64)
        hit = iota((64, n_rows), 0) + first == source
        order[pl.ds(first, 64), :] = jnp.where(hit, 1.0, 0.0).astype(BF)
        return carry

    lax.fori_loop(0, n_rows // 64, make_order, 0)
    loads[5].wait()
    hid_t[...] = nn(hid[...], order[...]).astype(BF)

    go_raw(ROUND4)

    def pack_block(i, carry):
        tile = raw[pl.ds(pl.multiple_of(i * tall + toks, 16), 16), 0:128].astype(F32)
        id0, id1 = tile[0:1, :], tile[1:2, :]
        routed = jnp.where((expert == id0) | (expert == id1), 1.0, 0.0)
        rank = jnp.where(routed > 0.0, nn(routed.astype(BF), upto) - 1.0, -1.0)
        chosen = jnp.concatenate(
            [jnp.where(rank[j:j + 1, :] == slot_no, 1.0, 0.0).astype(BF) for j in range(n_exp)], axis=0)
        rows = nn(chosen, raw[pl.ds(pl.multiple_of(i * tall, 16), toks), :]).astype(BF)
        for j in range(n_exp):
            raw_pack[j, pl.ds(pl.multiple_of(i * cap, 16), cap), :] = rows[j * cap:(j + 1) * cap, :]
        return carry

    lax.fori_loop(0, n_seq, pack_block, 0)
    cut = 512
    y_copies, y_recvs = [], []
    for part, (first, count) in enumerate([(0, cut), (cut, n_rows - cut)]):
        rows = pl.ds(first, count)
        y_recvs.append([])
        for i, rel in enumerate(REL[1:], 1):
            peer = exp_at(rel)
            there = REL_SLOT[((-rel[0] + 1) % NZ - 1, rel[1])]
            c = remote(
                raw_pack.at[peer, rows], x.at[rows, pl.ds(raw_at + there * RAW, RAW)],
                y_send.at[part, there], y_recv.at[part, there], {"exp": peer})
            c.start()
            y_copies.append(c)
            y_recvs[-1].append(remote(
                raw_pack.at[peer, rows], x.at[rows, pl.ds(raw_at + i * RAW, RAW)],
                y_send.at[part, i], y_recv.at[part, i], {"exp": peer}))
    x[:, raw_at:raw_at + RAW] = raw_pack[e]

    go(ROUND1[0])

    for c in a_copies:
        c.wait_recv()

    def gain_of(b):
        g3 = st_r[b, 128:144, :].astype(F32)
        return g3[0:1, :] + g3[1:2, :] + g3[2:3, :]

    def scan_up(b, state):
        res_s[b, 0:64, :] = state.astype(BF)
        return gain_of(b) * state + st_r[b, 0:64, :].astype(F32)

    def scan_down(i, state):
        b = n_seq - 1 - i
        res_s[b, 64:128, :] = state.astype(BF)
        return gain_of(b) * state + st_r[b, 64:128, :].astype(F32)

    zero = jnp.zeros((64, 128), F32)
    lax.fori_loop(0, n_seq, scan_up, zero)
    lax.fori_loop(0, n_seq, scan_down, zero)
    b_copies = []
    for off in range(1, n_seq):
        peer = (me + off) % n_seq
        b_copies.append(remote(res_s.at[peer], res_r.at[me], b_send.at[off], b_recv.at[off], {"seq": peer}))
        b_copies[-1].start()
    res_r[me] = res_s[me]

    for step in ROUND1[1:]:
        go(step)

    for c in b_copies:
        c.wait_recv()

    def finish_head(h, carry):
        row, col, total = head_terms(h)
        cols = pl.ds(pl.multiple_of(h * 128, 128), 128)
        q, k, v, g = qb[:, cols], kb[:, cols], vb[:, cols], gb[:, cols]
        two = res_r[pl.ds(2 * h, 2)]
        inc = two[:, 0:64, :].reshape(128, 128)
        upc = two[:, 64:128, :].reshape(128, 128)
        lead, tail = jnp.exp(col), jnp.exp(total - col)
        spread = jnp.broadcast_to(col, (128, 128)) - jnp.broadcast_to(row, (128, 128))
        causal = iota((128, 128), 0) >= iota((128, 128), 1)
        mask = jnp.exp(jnp.where(causal, spread, -jnp.inf))
        gs = nt(g, v) * mask
        qk = nt(q, k) * mask
        qo[:, cols] = (nn(gs.astype(BF), k) + lead * nt(g, inc)).astype(BF)
        ko[:, cols] = (nn(gs.T.astype(BF), q) + tail * nt(v, upc)).astype(BF)
        vo[:, cols] = (nn(qk.T.astype(BF), g) + tail * nn(k, upc)).astype(BF)
        return carry

    lax.fori_loop(0, heads, finish_head, 0)

    chunk = 1024
    chunks = width // chunk
    units = w.shape[0]

    def x_cols(i):
        return pl.ds(pl.multiple_of(i * chunk + jnp.where(i * chunk >= gate_at, 128, 0), 128), chunk)

    wide = gate_at // chunk

    def product(start, count, lo, hi):
        rows = pl.ds(start, count)
        if lo == 0:
            back[:, rows] = jnp.zeros((units, count), F32)

        def one(i, carry):
            cols = pl.ds(pl.multiple_of(i * chunk, chunk), chunk)
            back[:, rows] += nt(w[:, cols], x[rows, x_cols(i)])
            return carry

        lax.fori_loop(lo, hi, one, 0)

    def use_product(start, count):
        rows = pl.ds(start, count)
        first = jnp.where(iota((8, 128), 1) == 0, 1.0, 0.0).astype(BF)
        gate = nt(first, x[rows, gate_at:raw_at])[0:1, :]

        def after(i, total):
            part = pl.ds(pl.multiple_of(i * 64, 64), 64)
            b = back[part, rows]
            ho[part, rows] = (gate * b).astype(BF)
            return total + jnp.sum(b * hid_t[part, rows].astype(F32), axis=0, keepdims=True)

        total = lax.fori_loop(0, units // 64, after, jnp.zeros((1, count), F32))
        parts[0:1, rows] = total

    def scaled(start, count, cols):
        rows = pl.ds(start, count)
        gate = x[rows, gate_at:raw_at]
        return x[rows, cols] * jnp.concatenate([gate] * (chunk // 128), axis=1)

    p_copies = []
    parts_s[...] = jnp.zeros_like(parts_s)

    def hand_out(first, last):
        for i in range(first, last):
            parts_s[i, 0:1, 0:cap] = parts[0:1, i * cap:(i + 1) * cap]
            if i > 0:
                owner = {"seq": seq_at(OFFS[i])}
                c = remote(parts_s.at[i], parts_r.at[i], p_send.at[i], p_recv.at[i], owner)
                c.start()
                p_copies.append(c)

    def first_grad(i, carry):
        cols = pl.ds(pl.multiple_of(i * chunk, chunk), chunk)
        acc[:, cols] = nn(hid_t[:, 0:cut], scaled(0, cut, x_cols(i)))
        return carry

    for c in loads[7:]:
        c.wait()
    go(ROUND2[:6] + ROUND2[-1:])
    product(0, cut // 2, 0, wide)
    go(ROUND2[6:10])
    product(cut // 2, cut // 2, 0, wide)
    go(ROUND3)
    lax.fori_loop(0, wide, first_grad, 0)
    for c in y_recvs[0]:
        c.wait_recv()
    product(0, cut, wide, chunks)
    use_product(0, cut)
    hand_out(0, cut // cap)
    lax.fori_loop(wide, chunks, first_grad, 0)
    go(ROUND4)
    product(cut, n_rows - cut, 0, wide)
    for c in y_recvs[1]:
        c.wait_recv()
    product(cut, n_rows - cut, wide, chunks)
    use_product(cut, n_rows - cut)
    hand_out(cut // cap, n_seq)

    def last_grad(i, carry):
        cols = pl.ds(pl.multiple_of(i * chunk, chunk), chunk)
        wg[:, cols] = (acc[:, cols] + nn(hid_t[:, cut:], scaled(cut, n_rows - cut, x_cols(i)))).astype(BF)
        return carry

    lax.fori_loop(0, chunks, last_grad, 0)
    ho_out[...] = nt(ho[...], order[...]).astype(BF)

    total = parts_s[0]
    for i, c in enumerate(p_copies):
        c.wait_recv()
        total = total + parts_r[i + 1]
    per_tok = jnp.sum(sel[...] * to_col(total[0:1, :])[0:cap, :], axis=0, keepdims=True)
    tok_s[...] = jnp.broadcast_to(per_tok, (8, 128))
    t_copies = []
    for off in range(1, n_exp):
        peer = (e + off) % n_exp
        t_copies.append(remote(tok_s, tok_r.at[e], t_send.at[off], t_recv.at[off], {"exp": peer}))
        t_copies[-1].start()
    tok_r[e] = tok_s[...]
    for c in t_copies:
        c.wait_recv()
    for k in range(2):
        gate_out[k:k + 1, :] = sum(
            jnp.where(id_rows[k] == float(i), tok_r[i, 0:1, :], 0.0) for i in range(n_exp))

    for c in z_copies + y_copies + a_copies + b_copies + p_copies + t_copies:
        c.wait_send()
    for m in MSGS:
        message(m).wait_send()
    for m in RAW_MSGS:
        raw_message(m).wait_send()


def write_out(q_in, k_in, v_in, ho_in, wg_in, gate_in, q_out, k_out, v_out, ho_out, wg_out, gate_out, sem):
    e = lax.axis_index("exp")
    feat = wg_in.shape[1] // len(REL)
    thin = feat - RAW
    pairs = []
    for i, (z, core) in enumerate(REL):
        there = ((e // 2 + z + NZ) % NZ) * 2 + (e % 2 + core) % 2
        first = pl.multiple_of(there * feat, 128)
        pairs.append((wg_in.at[:, pl.ds(i * thin, thin)], wg_out.at[:, pl.ds(first, thin)]))
        raw_in = wg_in.at[:, pl.ds(len(REL) * thin + i * RAW, RAW)]
        pairs.append((raw_in, wg_out.at[:, pl.ds(first + thin, RAW)]))
    pairs += [(q_in, q_out), (k_in, k_out), (v_in, v_out), (ho_in, ho_out), (gate_in, gate_out)]
    copies = [pltpu.make_async_copy(a, b, sem.at[i]) for i, (a, b) in enumerate(pairs)]
    for c in copies:
        c.start()
    for c in copies:
        c.wait()


def on_device(
    queries, keys, values, attn_grad, log_decay, moe_grad, gate_probs, expert_ids, hidden_acts, down_weight
):
    n_seq, n_exp = lax.axis_size("seq"), lax.axis_size("exp")
    _, slots, units = hidden_acts.shape
    width = down_weight.shape[2]
    toks, flat = queries.shape
    feat = moe_grad.shape[1]
    hbm = pl.BlockSpec(memory_space=pl.ANY)
    vmem = pl.BlockSpec(memory_space=pltpu.VMEM)
    dma = pltpu.SemaphoreType.DMA
    V = pltpu.VMEM
    wide = V((toks, flat), BF)
    shapes = [
        ((toks, flat), BF), ((toks, flat), BF), ((toks, flat), BF),
        ((units, slots), BF), ((units, width), BF), ((2, toks), F32),
    ]
    held = pl.pallas_call(
        kernel,
        out_shape=tuple(V(*s) for s in shapes),
        in_specs=[hbm] * 7 + [vmem] * 3,
        out_specs=(vmem,) * 6,
        scratch_shapes=[
            wide, wide, wide, wide, V((toks, feat), BF),
            V((n_seq * (toks + 16), RAW), BF), V((n_exp, slots, RAW), BF), V((units, slots), BF), V((units, slots), BF), V((slots, slots), BF), V((units, width), BF),
            V((slots, width + 128), BF), V((n_exp * slots // n_seq, feat - RAW), BF),
            V((slots // n_seq, 128), F32), V((units, slots), F32), V((units, width), F32),
            V((units, slots), BF), V((8, slots), F32),
            V((n_seq, 8, 128), F32), V((n_seq, 8, 128), F32),
            V((8, 128), F32), V((n_exp, 8, 128), F32),
            V((n_seq, 144, 128), BF), V((n_seq, 144, 128), BF),
            V((n_seq, 128, 128), BF), V((n_seq, 128, 128), BF),
            V(log_decay.shape[::-1], F32),
            dma((7 + 2 * n_exp,)),
            dma((n_exp,)), dma((n_exp,)), dma((n_seq,)), dma((n_seq,)), dma((n_seq,)), dma((n_seq,)),
            dma((len(MSGS),)), dma((len(MSGS),)), dma((len(RAW_MSGS),)), dma((len(RAW_MSGS),)),
            dma((2, n_exp)), dma((2, n_exp)), dma((n_seq,)), dma((n_seq,)), dma((n_exp,)), dma((n_exp,)),
        ],
        compiler_params=pltpu.CompilerParams(
            collective_id=0, has_side_effects=True, vmem_limit_bytes=53 * 1024 * 1024
        ),
    )(
        queries, keys, values, attn_grad, moe_grad, hidden_acts[0].T, down_weight[0],
        log_decay.T, gate_probs.T, expert_ids.T,
    )
    out = pl.pallas_call(
        write_out,
        out_shape=tuple(jax.ShapeDtypeStruct(*s) for s in shapes),
        in_specs=[vmem] * 6,
        out_specs=(hbm,) * 6,
        scratch_shapes=[dma((5 + 2 * n_exp,))],
        compiler_params=pltpu.CompilerParams(vmem_limit_bytes=1024 * 1024),
    )(*held)
    return (*out[:3], out[3].T[None], out[4][None], out[5].T)


def solution(mesh):
    return jax.shard_map(
        on_device,
        mesh=mesh,
        in_specs=(
            P("seq", "exp"),
            P("seq", "exp"),
            P("seq", "exp"),
            P("seq", "exp"),
            P("seq", "exp"),
            P("seq", "exp"),
            P("seq", None),
            P("seq", None),
            P("exp", None, "seq"),
            P("exp", "seq", None),
        ),
        out_specs=(
            P("seq", "exp"),
            P("seq", "exp"),
            P("seq", "exp"),
            P("exp", None, "seq"),
            P("exp", "seq", None),
            P("seq", None),
        ),
        check_vma=False,
    )
```
